512 devices in a mesh: seq: 32 (over z, core), dp: 16 (over x, y).
Axes of the slice: x: 4, y: 4, z: 16, core: 2. Of those that a mesh axis runs over, the one named last changes fastest.
Arguments:
- queries: bfloat16 [16, 4096, 2048], P('dp', 'seq'), may hold values from -6 to 6
- key_rows: bfloat16 [16, 4096, 256], P('dp', 'seq'), may hold values from -6 to 6
- value_matrix: bfloat16 [16, 4096, 256], P('dp', 'seq'), may hold values from -6 to 6
- head_sink_logits: float32 [32], replicated, may hold values from 2 to 6
- residual: bfloat16 [16, 4096, 2880], P('dp', 'seq'), may hold values from -6 to 6
- out_weight: bfloat16 [2048, 2880], P('dp'), may hold values from -0.125 to 0.125
- norm_gain: float32 [2880], replicated, may hold values from 0.25 to 1.75
- router: bfloat16 [2880, 128], replicated, may hold values from -0.109375 to 0.109375
- expert_gate: bfloat16 [2880, 4096], P('dp', 'seq'), may hold values from -0.109375 to 0.109375
- expert_up: bfloat16 [2880, 4096], P('dp', 'seq'), may hold values from -0.109375 to 0.109375
- expert_down: bfloat16 [2880, 4096], P('dp', 'seq'), may hold values from -0.125 to 0.125
- routes: int32 [16, 4096, 4], P('dp', 'seq'), may hold values from 0 to 127, as said below
- group_ids: int32 [16], P('dp'), may hold values from 0 to 3, never falling along the last dimension, each value on 1 to 8 neighbouring positions
- rewards: int32 [16], P('dp'), may hold values from 0 to 3
- response_mask: int32 [16, 4096], P('dp', 'seq'), may hold values from 0 to 1, as said below
- upstream: bfloat16 [16, 4096, 2880], P('dp', 'seq'), may hold values from -6 to 6
Outputs:
- grad_queries: bfloat16 [16, 4096, 2048], P('dp', 'seq')
- grad_keys: bfloat16 [16, 4096, 256], P('dp', 'seq')
- grad_values: bfloat16 [16, 4096, 256], P('dp', 'seq')
- grad_residual: bfloat16 [16, 4096, 2880], P('dp', 'seq')
- grad_sinks: float32 [32], replicated
The draws below stay inside these ranges and needn't reach their ends.
Inputs may be any that keep to these rules, and one draw needn't show every extreme that they name: `routes`: each token names 4 different experts. Among the 128 positions of every aligned block of a rollout at most 4 tokens name a given expert below 2; the first block of the first rollout has exactly 4 for each of them. `group_ids`: the rollouts of one group are adjacent and every group has 1 to 8 rollouts. `response_mask`: in each rollout the ones form one run that starts within the first quarter of the positions and ends within the last quarter.
All inputs are finite; a program needn't handle non-finite values.
Results may differ from the reference program's by a relative error of at most 0.0095.
Values may be sent and summed in bfloat16 or wider, within the bound.
No kernel may reach another device: no remote copies, remote signals or barrier semaphores. Data moves between devices by JAX's collectives and lax.ppermute only.
A program may use at most 128 MiB of HBM per device.

```python
import math
from functools import partial
import jax
import jax.numpy as jnp
import numpy as np
from jax import lax

D = 2880
HEAD_SIZE = 64
WINDOW = 128
EXPERTS = 128
TOPK = 4
QUERY_HEADS = 32
KEY_VALUE_HEADS = 4
HID = 2048
EW = 2
CAP = 4
TOK_DEV = 128
ROLLOUT_LENGTH = 4096
ROLLOUT_COUNT = 16
NTOK = 65536
PIECES = 16
HID_DEV = 128
GROUPS = 4
GROUP_MOST = 8


def paired_fields(key):
    base = jax.random.fold_in(key, 5)
    query_random_seed, keys_random_seed = jax.random.split(base, 2)
    sampled_query = jnp.clip(jax.random.normal(query_random_seed, (ROLLOUT_COUNT, ROLLOUT_LENGTH, KEY_VALUE_HEADS, QUERY_HEADS // KEY_VALUE_HEADS, HEAD_SIZE), jnp.float32), -6.0, 6.0)
    sampled_keys = jnp.clip(jax.random.normal(keys_random_seed, (ROLLOUT_COUNT, ROLLOUT_LENGTH, KEY_VALUE_HEADS, HEAD_SIZE), jnp.float32), -6.0, 6.0)
    return (sampled_query.reshape(ROLLOUT_COUNT, ROLLOUT_LENGTH, QUERY_HEADS * HEAD_SIZE), sampled_keys.reshape(ROLLOUT_COUNT, ROLLOUT_LENGTH, KEY_VALUE_HEADS * HEAD_SIZE))


def draw_queries(key, part):
    return paired_fields(key)[0].astype(jnp.bfloat16)


def draw_key_rows(key, part):
    return paired_fields(key)[1].astype(jnp.bfloat16)


def draw_routes(key, part):
    base = jax.random.fold_in(key, 11)
    full_key, light_key, order_key, other_key = jax.random.split(base, 4)
    blocks = ROLLOUT_COUNT * (ROLLOUT_LENGTH // TOK_DEV)
    filled = jax.random.randint(full_key, (blocks, EW), 0, 4) == 0
    lighter = jax.random.randint(light_key, (blocks, EW), 0, 2)
    counts = jnp.where(filled, CAP, lighter)
    counts = jnp.where(jnp.arange(blocks)[:, None] == 0, CAP, counts)
    order_scores = jax.random.randint(order_key, (blocks, EW, TOK_DEV), 0, 1 << 20) * TOK_DEV + jnp.arange(TOK_DEV)
    order_rank = jnp.argsort(jnp.argsort(order_scores, axis=-1), axis=-1)
    chosen = order_rank < counts[:, :, None]
    other_scores = jax.random.randint(other_key, (blocks, TOK_DEV, EXPERTS - EW), 0, 1 << 20) * (EXPERTS - EW) + jnp.arange(EXPERTS - EW)
    others = lax.top_k(other_scores, TOPK)[1] + EW
    columns = []
    for place in range(TOPK):
        column = others[:, :, place]
        if place < EW:
            column = jnp.where(chosen[:, place, :], place, column)
        columns.append(column)
    return jnp.stack(columns, axis=-1).reshape(ROLLOUT_COUNT, ROLLOUT_LENGTH, TOPK).astype(jnp.int32)


def draw_response_mask(key, part):
    start_key, finish_key = jax.random.split(jax.random.fold_in(key, 13))
    opening = jax.random.randint(start_key, (ROLLOUT_COUNT, 1), 0, ROLLOUT_LENGTH // 4)
    closing = jax.random.randint(finish_key, (ROLLOUT_COUNT, 1), 3 * ROLLOUT_LENGTH // 4, ROLLOUT_LENGTH)
    position = jnp.arange(ROLLOUT_LENGTH)[None, :]
    return ((position >= opening) & (position <= closing)).astype(jnp.int32)


def set_ends(entries, key, low, high):
    spot = [jax.random.randint(jax.random.fold_in(key, axis), (), 0, length) for axis, length in enumerate(entries.shape)]
    main_axis = entries.shape.index(max(entries.shape))
    neighbour = spot[:main_axis] + [(spot[main_axis] + 1) % entries.shape[main_axis]] + spot[main_axis + 1:]
    return entries.at[tuple(spot)].set(low).at[tuple(neighbour)].set(high)


def steps_of(own_key, shape, cuts, low, high):
    factor_of, own = 1.0, jax.random.fold_in(own_key, 6)
    for axis_at, shards_of in cuts:
        draws = jnp.exp(jax.random.uniform(jax.random.fold_in(own, axis_at), (shards_of,), jnp.float32, low / len(cuts), high / len(cuts)))
        factor_of = factor_of * jnp.repeat(draws, shape[axis_at] // shards_of).reshape([-1 if axis == axis_at else 1 for axis in range(len(shape))])
    return factor_of


def length_profile(count, total, reach, skew):
    weights = [(1 << 20) // math.isqrt(rank ** skew) + 1 for rank in range(2, count + 1)]
    surplus, holding = total - reach - (count - 1), [1] * (count - 1)
    while surplus > 0:
        candidates = [i for i in range(count - 1) if holding[i] < reach]
        whole, remaining = sum([weights[i] for i in candidates]), surplus
        for i in candidates:
            more = min(reach - holding[i], max(1, remaining * weights[i] // whole), surplus)
            holding[i] = holding[i] + more
            surplus = surplus - more
    return np.array([reach] + holding)


def uneven(key, amount, total, most, lean):
    if amount == 2:
        one = jax.random.randint(key, (), max(1, total - most), min(most, total - 1) + 1)
        return jnp.stack([one, total - one])
    sizes = jnp.asarray(length_profile(amount, total, most, lean), jnp.int32)
    twos = (amount - 1) // 2
    donor, receiver = sizes[1:1 + 2 * twos:2], sizes[2:2 + 2 * twos:2]
    room = jnp.minimum(donor - 1, most - receiver)
    moved = jax.random.randint(jax.random.fold_in(key, 1), (twos,), 0, 1 << 20) % (room + 1)
    sizes = sizes.at[1:1 + 2 * twos:2].set(donor - moved).at[2:2 + 2 * twos:2].set(receiver + moved)
    return sizes[jax.random.permutation(jax.random.fold_in(key, 2), amount)]


def noise(rng, extent, deviation, bound, cuts=(), kind=jnp.bfloat16):
    drawn = jax.random.normal(rng, extent, jnp.float32) * deviation
    if len(cuts) > 0:
        drawn = steps_of(rng, extent, cuts, -0.22, 0.18) * drawn
    return jnp.clip(drawn, min=-bound, max=bound).astype(kind)


def setup_inputs(seed: int = 0) -> dict:
    streams_of = jax.random.split(jax.random.key(seed), 17)
    queries = draw_queries(jax.random.fold_in(streams_of[16], 71), 0)
    key_rows = draw_key_rows(jax.random.fold_in(streams_of[16], 71), 0)
    value_matrix = noise(streams_of[2], (ROLLOUT_COUNT, ROLLOUT_LENGTH, KEY_VALUE_HEADS * HEAD_SIZE), 1.0, 6.0, ((0, 16), (1, 32)))
    head_sink_logits = jnp.clip(jax.random.uniform(streams_of[3], (QUERY_HEADS,), jnp.float32, 2.0, 6.0), 2.0, 6.0)
    residual = noise(streams_of[4], (ROLLOUT_COUNT, ROLLOUT_LENGTH, D), 1.0, 6.0, ((0, 16), (1, 32)))
    out_weight = noise(streams_of[5], (QUERY_HEADS * HEAD_SIZE, D), (QUERY_HEADS * HEAD_SIZE) ** -0.5, 0.125, ((0, 16),))
    norm_gain = jnp.clip(1.0 + 0.15 * jax.random.normal(streams_of[6], (D,), jnp.float32), 0.25, 1.75)
    router = noise(streams_of[7], (D, EXPERTS), D ** -0.5, 0.109375)
    expert_gate = noise(streams_of[8], (D, EW * HID), D ** -0.5, 0.109375, ((0, 16), (1, 32)))
    expert_up = noise(streams_of[9], (D, EW * HID), D ** -0.5, 0.109375, ((0, 16), (1, 32)))
    expert_down = noise(streams_of[10], (D, EW * HID), HID ** -0.5, 0.125, ((0, 16), (1, 32)))
    routes = draw_routes(jax.random.fold_in(streams_of[16], 71), 0)
    group_ids = jnp.searchsorted(jnp.cumsum(uneven(streams_of[12], GROUPS, ROLLOUT_COUNT, GROUP_MOST, 0)), jnp.arange(ROLLOUT_COUNT), side="right").astype(jnp.int32)
    rewards = set_ends(jax.random.randint(streams_of[13], (ROLLOUT_COUNT,), 0, 4), jax.random.fold_in(streams_of[13], 1), 0, 3).astype(jnp.int32)
    response_mask = draw_response_mask(jax.random.fold_in(streams_of[16], 71), 0)
    upstream = noise(streams_of[15], (ROLLOUT_COUNT, ROLLOUT_LENGTH, D), 1.0, 6.0, ((0, 16), (1, 32)))
    return {"queries": queries, "key_rows": key_rows, "value_matrix": value_matrix, "head_sink_logits": head_sink_logits, "residual": residual, "out_weight": out_weight, "norm_gain": norm_gain, "router": router, "expert_gate": expert_gate, "expert_up": expert_up, "expert_down": expert_down, "routes": routes, "group_ids": group_ids, "rewards": rewards, "response_mask": response_mask, "upstream": upstream}


NORM_EPS = 1e-05
GLU_SLOPE = 1.702
HIGHEST = lax.Precision.HIGHEST

def rounded(values):
    return lax.optimization_barrier(values.astype(jnp.bfloat16))

def glu_forward(gate_pre, up_pre):
    return rounded((up_pre + 1.0) * gate_pre * jax.nn.sigmoid(GLU_SLOPE * gate_pre))

def glu_grads(grad_act, gate_pre, up_pre):
    sigmoid_gate = jax.nn.sigmoid(GLU_SLOPE * gate_pre)
    grad_up = grad_act * (gate_pre * sigmoid_gate)
    grad_gate = grad_act * (up_pre + 1.0) * (sigmoid_gate + GLU_SLOPE * gate_pre * sigmoid_gate * (1.0 - sigmoid_gate))
    return (grad_gate, grad_up)

def head_scores(query_tile_block, key_tile_block, head_sink_logits, allowed):
    query_total_count = query_tile_block.shape[0]
    key_total_count = key_tile_block.shape[0]
    query_head_rows = query_tile_block.reshape(query_total_count, KEY_VALUE_HEADS, QUERY_HEADS // KEY_VALUE_HEADS, HEAD_SIZE).astype(jnp.float32)
    key_head_rows = key_tile_block.reshape(key_total_count, KEY_VALUE_HEADS, HEAD_SIZE).astype(jnp.float32)
    attention_scores = jnp.einsum('baqj,eaj->aqbe', query_head_rows, key_head_rows) * HEAD_SIZE ** (-0.5)
    attention_scores = jnp.where(allowed[None, None], attention_scores, -1e+30)
    sink_logit_column = head_sink_logits.reshape(KEY_VALUE_HEADS, QUERY_HEADS // KEY_VALUE_HEADS)[:, :, None]
    largest = jnp.maximum(lax.optimization_barrier(jnp.max(attention_scores, axis=3)), sink_logit_column)
    raised = jnp.where(allowed[None, None], jnp.exp(attention_scores - largest[..., None]), 0.0)
    sink_raised = jnp.exp(sink_logit_column - largest)
    denominator = lax.optimization_barrier(jnp.sum(raised, axis=3)) + sink_raised
    return (raised / denominator[..., None], sink_raised / denominator)

def head_mix(reduced_probabilities, value_tile_block):
    key_total_count = value_tile_block.shape[0]
    value_head_rows = value_tile_block.reshape(key_total_count, KEY_VALUE_HEADS, HEAD_SIZE).astype(jnp.float32)
    mixed_output = jnp.einsum('amlh,hai->lami', reduced_probabilities.astype(jnp.float32), value_head_rows)
    return rounded(mixed_output.reshape(mixed_output.shape[0], QUERY_HEADS * HEAD_SIZE))

def head_grads(probs, reduced_probabilities, sink_probs, query_tile_block, key_tile_block, value_tile_block, mixed_gradient):
    query_total_count = query_tile_block.shape[0]
    key_total_count = key_tile_block.shape[0]
    query_head_rows = query_tile_block.reshape(query_total_count, KEY_VALUE_HEADS, QUERY_HEADS // KEY_VALUE_HEADS, HEAD_SIZE).astype(jnp.float32)
    key_head_rows = key_tile_block.reshape(key_total_count, KEY_VALUE_HEADS, HEAD_SIZE).astype(jnp.float32)
    value_head_rows = value_tile_block.reshape(key_total_count, KEY_VALUE_HEADS, HEAD_SIZE).astype(jnp.float32)
    heads_gradient = mixed_gradient.reshape(query_total_count, KEY_VALUE_HEADS, QUERY_HEADS // KEY_VALUE_HEADS, HEAD_SIZE).astype(jnp.float32)
    probability_gradient = jnp.einsum('baqj,eaj->aqbe', heads_gradient, value_head_rows)
    spread = lax.optimization_barrier(jnp.sum(probs * probability_gradient, axis=3))
    score_gradient = rounded(probs * (probability_gradient - spread[..., None])).astype(jnp.float32)
    head_scaling = HEAD_SIZE ** (-0.5)
    query_gradient = jnp.einsum('amlh,hai->lami', score_gradient, key_head_rows) * head_scaling
    key_gradient = jnp.einsum('ujko,kujm->oum', score_gradient, query_head_rows) * head_scaling
    value_gradient = jnp.einsum('ujko,kujm->oum', reduced_probabilities.astype(jnp.float32), heads_gradient)
    sink_gradient = -lax.optimization_barrier(jnp.sum(sink_probs * spread, axis=2)).reshape(QUERY_HEADS)
    return (query_gradient.reshape(query_total_count, QUERY_HEADS * HEAD_SIZE).astype(jnp.bfloat16), key_gradient.reshape(key_total_count, KEY_VALUE_HEADS * HEAD_SIZE), value_gradient.reshape(key_total_count, KEY_VALUE_HEADS * HEAD_SIZE), sink_gradient)

def fold_keys(parts):
    own_part = parts[:, WINDOW:]
    halo_part = parts[:, :WINDOW]
    from_next = jnp.concatenate([halo_part[1:], jnp.zeros_like(halo_part[:1])], axis=0)
    tail_rows = own_part[:, TOK_DEV - WINDOW:] + from_next
    merged = jnp.concatenate([own_part[:, :TOK_DEV - WINDOW], tail_rows], axis=1)
    return merged.reshape(ROLLOUT_LENGTH, parts.shape[2])

def one_rollout(head_sink_logits, out_weight, norm_gain, router, expert_gate, expert_up, expert_down, packed):
    queries, key_rows, value_matrix, residual, mask_row, route_rows, upstream, token_scale = packed
    blocks = ROLLOUT_LENGTH // TOK_DEV
    block_ids = jnp.arange(blocks, dtype=jnp.int32)
    key_padded = jnp.concatenate([jnp.zeros((WINDOW, key_rows.shape[1]), key_rows.dtype), key_rows], axis=0)
    value_padded = jnp.concatenate([jnp.zeros((WINDOW, value_matrix.shape[1]), value_matrix.dtype), value_matrix], axis=0)
    row_index = jnp.arange(TOK_DEV, dtype=jnp.int32)[:, None]
    col_index = jnp.arange(WINDOW + TOK_DEV, dtype=jnp.int32)[None, :]
    in_window = (col_index >= row_index + 1) & (col_index <= row_index + WINDOW)

    def block_probs(block_id):
        offset = block_id * TOK_DEV
        query_tile_block = lax.dynamic_slice_in_dim(queries, offset, TOK_DEV, 0)
        key_tile_block = lax.dynamic_slice_in_dim(key_padded, offset, WINDOW + TOK_DEV, 0)
        value_tile_block = lax.dynamic_slice_in_dim(value_padded, offset, WINDOW + TOK_DEV, 0)
        allowed = in_window & ((col_index >= WINDOW) | (block_id > 0))
        probs, sink_probs = head_scores(query_tile_block, key_tile_block, head_sink_logits, allowed)
        return (probs, sink_probs, query_tile_block, key_tile_block, value_tile_block)

    def block_forward(block_id):
        probs, sink_probs, query_tile_block, key_tile_block, value_tile_block = block_probs(block_id)
        return head_mix(rounded(probs), value_tile_block)
    attended = lax.map(block_forward, block_ids).reshape(ROLLOUT_LENGTH, QUERY_HEADS * HEAD_SIZE)
    projected = jnp.dot(attended, out_weight, preferred_element_type=jnp.float32)
    mid_rows = rounded(residual.astype(jnp.float32) + projected)
    mid_wide = mid_rows.astype(jnp.float32)
    inv_rms = lax.rsqrt(lax.optimization_barrier(jnp.mean(mid_wide * mid_wide, axis=1, keepdims=True)) + NORM_EPS)
    unit_rows = mid_wide * inv_rms
    normed = rounded(unit_rows * norm_gain[None, :])
    logits = jnp.dot(normed, router, preferred_element_type=jnp.float32)
    route_logits = jnp.take_along_axis(logits, route_rows, axis=1)
    raised = jnp.exp(route_logits)
    route_weights = raised / lax.optimization_barrier(jnp.sum(raised, axis=1, keepdims=True))
    route_hot = route_rows[:, :, None] == jnp.arange(EXPERTS, dtype=jnp.int32)[None, None, :]
    member = route_hot[:, :, :EW]
    expert_share = lax.optimization_barrier(jnp.sum(jnp.where(member, route_weights[:, :, None], 0.0), axis=1))
    chosen = jnp.any(member, axis=1).reshape(blocks, TOK_DEV, EW)
    slot_rank = jnp.cumsum(chosen.astype(jnp.int32), axis=1) - 1
    slot_wide = (chosen[..., None] & (slot_rank[..., None] == jnp.arange(CAP, dtype=jnp.int32))).astype(jnp.float32)
    slot_rows = rounded(jnp.einsum('btec,btd->becd', slot_wide, normed.reshape(blocks, TOK_DEV, D).astype(jnp.float32), precision=HIGHEST))
    loss_weight = token_scale * mask_row.astype(jnp.float32)
    upstream_slots = jnp.einsum('btec,btd->becd', slot_wide, upstream.reshape(blocks, TOK_DEV, D).astype(jnp.float32), precision=HIGHEST)
    weight_slots = jnp.einsum('btec,bt->bec', slot_wide, loss_weight.reshape(blocks, TOK_DEV), precision=HIGHEST)
    share_slots = jnp.einsum('btec,bte->bec', slot_wide, expert_share.reshape(blocks, TOK_DEV, EW), precision=HIGHEST)
    cot_slots = weight_slots[..., None] * upstream_slots
    grad_share_parts = []
    grad_normed_moe = jnp.zeros((ROLLOUT_LENGTH, D), jnp.float32)
    for expert in range(EW):
        gate_cols = expert_gate[:, expert * HID:(expert + 1) * HID]
        up_cols = expert_up[:, expert * HID:(expert + 1) * HID]
        down_cols = expert_down[:, expert * HID:(expert + 1) * HID]
        flat_rows = slot_rows[:, expert].reshape(blocks * CAP, D)
        gate_pre = jnp.dot(flat_rows, gate_cols, preferred_element_type=jnp.float32)
        up_pre = jnp.dot(flat_rows, up_cols, preferred_element_type=jnp.float32)
        activation = glu_forward(gate_pre, up_pre)
        down_pieces = down_cols.reshape(D, PIECES, HID_DEV).astype(jnp.float32)
        partial_out = rounded(jnp.einsum('nph,dph->npd', activation.reshape(-1, PIECES, HID_DEV).astype(jnp.float32), down_pieces))
        expert_out = lax.optimization_barrier(jnp.sum(partial_out.astype(jnp.float32), axis=1)).reshape(blocks, CAP, D)
        expert_cot = cot_slots[:, expert]
        grad_share_parts.append(lax.optimization_barrier(jnp.sum(expert_cot * expert_out, axis=2)))
        grad_out = rounded(share_slots[:, expert, :, None] * expert_cot).reshape(blocks * CAP, D)
        grad_act = jnp.dot(grad_out, down_cols, preferred_element_type=jnp.float32)
        grad_gate, grad_up = glu_grads(grad_act, gate_pre, up_pre)
        gate_pieces = gate_cols.reshape(D, PIECES, HID_DEV).astype(jnp.float32)
        up_pieces = up_cols.reshape(D, PIECES, HID_DEV).astype(jnp.float32)
        gate_low = rounded(grad_gate).reshape(-1, PIECES, HID_DEV).astype(jnp.float32)
        up_low = rounded(grad_up).reshape(-1, PIECES, HID_DEV).astype(jnp.float32)
        grad_piece = rounded(jnp.einsum('nph,dph->npd', gate_low, gate_pieces) + jnp.einsum('nph,dph->npd', up_low, up_pieces))
        grad_rows = lax.optimization_barrier(jnp.sum(grad_piece.astype(jnp.float32), axis=1)).reshape(blocks, CAP, D)
        grad_normed_moe = grad_normed_moe + jnp.einsum('btc,bcd->btd', slot_wide[:, :, expert], grad_rows, precision=HIGHEST).reshape(ROLLOUT_LENGTH, D)
    grad_share_slots = jnp.stack(grad_share_parts, axis=1)
    grad_share = jnp.einsum('btec,bec->bte', slot_wide, grad_share_slots, precision=HIGHEST).reshape(ROLLOUT_LENGTH, EW)
    grad_weights = lax.optimization_barrier(jnp.sum(jnp.where(member, grad_share[:, None, :], 0.0), axis=2))
    grad_route = route_weights * (grad_weights - lax.optimization_barrier(jnp.sum(route_weights * grad_weights, axis=1, keepdims=True)))
    grad_logits = rounded(lax.optimization_barrier(jnp.sum(jnp.where(route_hot, grad_route[:, :, None], 0.0), axis=1)))
    grad_normed = jnp.dot(grad_logits, router.T, preferred_element_type=jnp.float32) + grad_normed_moe
    grad_unit = grad_normed * norm_gain[None, :]
    grad_mid = loss_weight[:, None] * upstream.astype(jnp.float32) + inv_rms * (grad_unit - unit_rows * lax.optimization_barrier(jnp.mean(grad_unit * unit_rows, axis=1, keepdims=True)))
    grad_residual = grad_mid.astype(jnp.bfloat16)
    grad_attended = jnp.dot(grad_residual, out_weight.T, preferred_element_type=jnp.float32).astype(jnp.bfloat16)

    def block_backward(block_id):
        probs, sink_probs, query_tile_block, key_tile_block, value_tile_block = block_probs(block_id)
        grad_block = lax.dynamic_slice_in_dim(grad_attended, block_id * TOK_DEV, TOK_DEV, 0)
        return head_grads(probs, rounded(probs), sink_probs, query_tile_block, key_tile_block, value_tile_block, grad_block)
    query_gradient, key_gradient, value_gradient, sink_gradient = lax.map(block_backward, block_ids)
    return (query_gradient.reshape(ROLLOUT_LENGTH, QUERY_HEADS * HEAD_SIZE), fold_keys(key_gradient).astype(jnp.bfloat16), fold_keys(value_gradient).astype(jnp.bfloat16), grad_residual, lax.optimization_barrier(jnp.sum(sink_gradient, axis=0)))

def reference(queries, key_rows, value_matrix, head_sink_logits, residual, out_weight, norm_gain, router, expert_gate, expert_up, expert_down, routes, group_ids, rewards, response_mask, upstream):
    group_hot = (group_ids[:, None] == jnp.arange(GROUPS, dtype=jnp.int32)[None, :]).astype(jnp.float32)
    reward = rewards.astype(jnp.float32)
    reward_terms = jnp.stack([jnp.ones_like(reward), reward, reward * reward], axis=1)
    group_totals = lax.optimization_barrier(jnp.sum(group_hot[:, :, None] * reward_terms[:, None, :], axis=0))
    group_sizes = group_totals[:, 0]
    group_means = group_totals[:, 1] / group_sizes
    group_spread = group_totals[:, 2] / group_sizes - group_means * group_means
    own_mean = lax.optimization_barrier(jnp.sum(group_hot * group_means[None, :], axis=1))
    own_spread = lax.optimization_barrier(jnp.sum(group_hot * group_spread[None, :], axis=1))
    advantage = (reward - own_mean) / jnp.sqrt(jnp.maximum(own_spread, 1.0))
    token_total = jnp.sum(response_mask.astype(jnp.float32))
    token_scale = -advantage * NTOK / token_total
    stepper = partial(one_rollout, head_sink_logits, out_weight, norm_gain, router, expert_gate, expert_up, expert_down)
    grads = lax.map(stepper, (queries, key_rows, value_matrix, residual, response_mask, routes, upstream, token_scale))
    return (grads[0], grads[1], grads[2], grads[3], lax.optimization_barrier(jnp.sum(grads[4], axis=0)))
```

```python
import jax
import jax.numpy as jnp
from jax import lax
from jax.sharding import Mesh, PartitionSpec as P

D = 2880
PADDED = 2944
HEAD_SIZE = 64
WINDOW = 128
EXPERTS = 128
QUERY_HEADS = 32
KEY_VALUE_HEADS = 4
EW = 2
CAP = 4
SLOTS = EW * CAP

NORM_EPS = 1e-05
GLU_SLOPE = 1.702
HIGHEST = lax.Precision.HIGHEST
CONTRACT_LAST = (((1,), (1,)), ((), ()))
F32 = jnp.float32
BF16 = jnp.bfloat16


def dot32(a, b, **kw):
    return jnp.dot(a, b, preferred_element_type=F32, **kw)


def dot_last(a, b):
    return lax.dot_general(a, b, CONTRACT_LAST, preferred_element_type=F32)


def exchange(value, axis):
    return lax.all_to_all(value, axis, split_axis=0, concat_axis=0, tiled=True)


def to_all(value, axis):
    count = lax.axis_size(axis)
    return exchange(jnp.broadcast_to(value[None], (count, *value.shape)), axis)


def swap_cores(value):
    return lax.ppermute(value, "core", [(0, 1), (1, 0)])


def along_seq(value, steps):
    chips, cores = lax.axis_size("z"), lax.axis_size("core")
    count = chips * cores
    first, last = max(0, -steps), min(count, count - steps)
    return lax.ppermute(value, ("z", "core"), [(i, i + steps) for i in range(first, last)])


def head_scores(query_rows, key_rows, sinks, allowed):
    tokens, keys = query_rows.shape[0], key_rows.shape[0]
    per_group = QUERY_HEADS // KEY_VALUE_HEADS
    q = query_rows.reshape(tokens, KEY_VALUE_HEADS, per_group, HEAD_SIZE)
    k = key_rows.reshape(keys, KEY_VALUE_HEADS, HEAD_SIZE)
    scores = jnp.einsum("baqj,eaj->aqbe", q, k, preferred_element_type=F32) * HEAD_SIZE**-0.5
    scores = jnp.where(allowed[None, None], scores, -1e30)
    sink_column = sinks.reshape(KEY_VALUE_HEADS, per_group)[:, :, None]
    largest = jnp.maximum(jnp.max(scores, axis=3), sink_column)
    raised = jnp.where(allowed[None, None], jnp.exp(scores - largest[..., None]), 0.0)
    sink_raised = jnp.exp(sink_column - largest)
    denominator = jnp.sum(raised, axis=3) + sink_raised
    return raised / denominator[..., None], sink_raised / denominator


def head_mix(probs_low, value_rows):
    v = value_rows.reshape(value_rows.shape[0], KEY_VALUE_HEADS, HEAD_SIZE)
    mixed = jnp.einsum("amlh,hai->lami", probs_low, v, preferred_element_type=F32)
    return mixed.reshape(mixed.shape[0], QUERY_HEADS * HEAD_SIZE).astype(BF16)


def head_grads(probs, probs_low, sink_probs, query_rows, key_rows, value_rows, grad_attended):
    tokens, keys = query_rows.shape[0], key_rows.shape[0]
    per_group = QUERY_HEADS // KEY_VALUE_HEADS
    q = query_rows.reshape(tokens, KEY_VALUE_HEADS, per_group, HEAD_SIZE)
    k = key_rows.reshape(keys, KEY_VALUE_HEADS, HEAD_SIZE)
    v = value_rows.reshape(keys, KEY_VALUE_HEADS, HEAD_SIZE)
    g = grad_attended.reshape(tokens, KEY_VALUE_HEADS, per_group, HEAD_SIZE)
    grad_prob = jnp.einsum("baqj,eaj->aqbe", g, v, preferred_element_type=F32)
    spread = jnp.sum(probs * grad_prob, axis=3)
    grad_score = (probs * (grad_prob - spread[..., None])).astype(BF16)
    scaling = HEAD_SIZE**-0.5
    grad_q = jnp.einsum("amlh,hai->lami", grad_score, k, preferred_element_type=F32) * scaling
    grad_k = jnp.einsum("ujko,kujm->oum", grad_score, q, preferred_element_type=F32) * scaling
    grad_v = jnp.einsum("ujko,kujm->oum", probs_low, g, preferred_element_type=F32)
    grad_sinks = -jnp.sum(sink_probs * spread, axis=2).reshape(QUERY_HEADS)
    return (
        grad_q.reshape(tokens, QUERY_HEADS * HEAD_SIZE).astype(BF16),
        grad_k.reshape(keys, KEY_VALUE_HEADS * HEAD_SIZE),
        grad_v.reshape(keys, KEY_VALUE_HEADS * HEAD_SIZE),
        grad_sinks,
    )


def shards(
    queries,
    key_rows,
    value_matrix,
    head_sink_logits,
    residual,
    out_weight,
    norm_gain,
    router,
    expert_gate,
    expert_up,
    expert_down,
    routes,
    group_ids,
    rewards,
    response_mask,
    upstream,
):
    chips, cores, dp_count = lax.axis_size("z"), lax.axis_size("core"), lax.axis_size("dp")
    core = lax.axis_index("core")
    seq_index = lax.axis_index("z") * cores + core
    query_rows = queries[0]
    tokens = query_rows.shape[0]
    group_count = max(dp_count // 4, 1)
    all_tokens = dp_count * chips * cores * tokens
    half = D // 2
    lanes = out_weight.shape[0]

    route_rows = routes[0]
    window = jnp.arange(EW, dtype=jnp.int32)
    chosen = jnp.any(route_rows[:, :, None] == window, axis=1)
    below = jnp.arange(tokens)[:, None] >= jnp.arange(tokens)[None, :]
    rank = dot32(below.astype(BF16), chosen.astype(BF16)) - 1.0
    slot_hot = chosen.T[:, None, :] & (
        rank.T[:, None, :] == jnp.arange(CAP, dtype=F32)[None, :, None]
    )
    pick = slot_hot.reshape(SLOTS, tokens)
    pick_low = pick.astype(BF16)
    slot_expert = jnp.repeat(window, CAP)
    upstream_slots = dot32(pick_low, upstream[0]).astype(BF16)
    residual_slots = dot32(pick_low, residual[0])

    shard = jnp.stack([expert_gate, expert_up, expert_down])
    gathered = to_all(shard, "dp")
    own_block = jnp.concatenate([gathered[:, i].reshape(D, -1) for i in range(3)], axis=1)
    other_block = swap_cores(own_block)
    hid = expert_gate.shape[1]

    by_expert = upstream_slots.reshape(EW, 1, CAP, D)
    outgoing = jnp.broadcast_to(by_expert, (EW, chips // EW, CAP, D)).reshape(chips, CAP, D)
    up_rows = exchange(outgoing, "z").reshape(chips * CAP, D)

    halo = along_seq(jnp.concatenate([key_rows[0], value_matrix[0]], axis=1), 1)
    kv_width = key_rows.shape[2]
    keys_here = jnp.concatenate([halo[:, :kv_width], key_rows[0]], axis=0)
    values_here = jnp.concatenate([halo[:, kv_width:], value_matrix[0]], axis=0)
    row_index = jnp.arange(tokens, dtype=jnp.int32)[:, None]
    col_index = jnp.arange(WINDOW + tokens, dtype=jnp.int32)[None, :]
    allowed = (
        (col_index >= row_index + 1)
        & (col_index <= row_index + WINDOW)
        & ((col_index >= WINDOW) | (seq_index > 0))
    )
    probs, sink_probs = head_scores(query_rows, keys_here, head_sink_logits, allowed)
    probs_low = probs.astype(BF16)
    attended = head_mix(probs_low, values_here)
    attended_slots = dot32(pick_low, attended).astype(BF16)

    mask_wide = response_mask[0].astype(F32)
    facts = jnp.stack(
        [
            jnp.sum(mask_wide),
            rewards[0].astype(F32),
            group_ids[0].astype(F32),
        ]
    )
    facts_row = jnp.pad(facts, (0, lanes - 3))[None].astype(BF16)
    columns = attended_slots.reshape(SLOTS, dp_count, lanes).transpose(1, 0, 2)
    sent = jnp.concatenate(
        [columns, jnp.broadcast_to(facts_row[None], (dp_count, 1, lanes))], axis=1
    )
    sent = jnp.pad(sent, ((0, 0), (0, 2 * SLOTS - SLOTS - 1), (0, 0)))
    arrived = exchange(sent, "dp")
    facts_all = arrived[:, SLOTS, :3].astype(F32)
    partial = dot32(arrived[:, :SLOTS].reshape(dp_count * SLOTS, lanes), out_weight)
    partial = exchange(partial.astype(BF16).reshape(dp_count, SLOTS, D), "dp")
    projected = jnp.sum(partial.astype(F32), axis=0)

    own_half = lax.dynamic_slice_in_dim(out_weight, core * half, half, axis=1)
    own_out = to_all(own_half, "dp").reshape(dp_count * lanes, half)
    other_out = swap_cores(own_out)

    mid = (residual_slots + projected).astype(BF16)
    mid_wide = lax.optimization_barrier(mid).astype(F32)
    inv_rms = lax.rsqrt(jnp.mean(mid_wide * mid_wide, axis=1, keepdims=True) + NORM_EPS)
    unit_rows = mid_wide * inv_rms
    normed = (unit_rows * norm_gain[None, :]).astype(BF16)

    counts_here = jnp.sum(facts_all[:, 0])
    group_hot = (facts_all[:, 2][:, None] == jnp.arange(group_count, dtype=F32)).astype(F32)
    reward_all = facts_all[:, 1]
    group_sizes = jnp.sum(group_hot, axis=0)
    group_sums = jnp.sum(group_hot * reward_all[:, None], axis=0)
    group_squares = jnp.sum(group_hot * (reward_all * reward_all)[:, None], axis=0)
    own_hot = (group_ids[0] == jnp.arange(group_count, dtype=jnp.int32)).astype(F32)
    means = group_sums / group_sizes
    spreads = group_squares / group_sizes - means * means
    own_mean = jnp.sum(jnp.where(own_hot > 0, means, 0.0))
    own_spread = jnp.sum(jnp.where(own_hot > 0, spreads, 0.0))
    advantage = (rewards[0].astype(F32) - own_mean) / jnp.sqrt(jnp.maximum(own_spread, 1.0))

    count_high = jnp.floor(counts_here / 64.0)
    count_tail = jnp.stack([count_high, counts_here - 64.0 * count_high])
    count_tail = jnp.pad(count_tail, (0, PADDED - D - 2)).astype(BF16)
    with_tail = jnp.concatenate(
        [normed, jnp.broadcast_to(count_tail[None], (SLOTS, PADDED - D))], axis=1
    )
    by_expert = with_tail.reshape(EW, 1, CAP, PADDED)
    outgoing = jnp.broadcast_to(by_expert, (EW, chips // EW, CAP, PADDED))
    came = exchange(outgoing.reshape(chips, CAP, PADDED), "z")
    count_parts = jnp.sum(came[:, 0, D : D + 2].astype(F32), axis=0)
    core_count = count_parts[0] * 64.0 + count_parts[1]
    token_total = core_count + swap_cores(jnp.full((8, 128), core_count))[0, 0]
    token_scale = -advantage * all_tokens / token_total
    loss_weight = token_scale * mask_wide

    rows = came.reshape(chips * CAP, PADDED)[:, :D]
    pieces = []
    shares = 0.0
    grads = []
    for block in (own_block, other_block):
        pre = dot32(rows, block[:, : 2 * hid])
        up_down = dot32(up_rows, block[:, 2 * hid :])
        gate_pre, up_pre = pre[:, :hid], pre[:, hid:]
        sigmoid_gate = jax.nn.sigmoid(GLU_SLOPE * gate_pre)
        activation = ((up_pre + 1.0) * gate_pre * sigmoid_gate).astype(BF16)
        shares = shares + jnp.sum(activation.astype(F32) * up_down, axis=1)
        grad_up = up_down * (gate_pre * sigmoid_gate)
        grad_gate = (
            up_down
            * (up_pre + 1.0)
            * (sigmoid_gate + GLU_SLOPE * gate_pre * sigmoid_gate * (1.0 - sigmoid_gate))
        )
        grads.append(jnp.concatenate([grad_gate, grad_up], axis=1).astype(BF16))
    piece = dot_last(grads[0], own_block[:, : 2 * hid]) + dot_last(grads[1], other_block[:, : 2 * hid])
    share_1 = shares.astype(BF16).astype(F32)
    share_2 = (shares - share_1).astype(BF16).astype(F32)
    share_3 = shares - share_1 - share_2
    tail = jnp.pad(jnp.stack([share_1, share_2, share_3], axis=1), ((0, 0), (0, PADDED - D - 3)))
    back = jnp.concatenate([piece, tail], axis=1).astype(BF16)
    back = exchange(back.reshape(chips, CAP, PADDED), "z")
    summed = jnp.sum(back.reshape(EW, chips // EW, CAP, PADDED).astype(F32), axis=1)
    summed = summed.reshape(SLOTS, PADDED)
    share_slots = jnp.sum(summed[:, D : D + 3], axis=1)

    logits = dot32(normed, router)
    route_slots = dot32(pick_low, route_rows.astype(BF16)).astype(jnp.int32)
    route_hot = route_slots[:, :, None] == jnp.arange(EXPERTS, dtype=jnp.int32)
    route_logits = jnp.sum(jnp.where(route_hot, logits[:, None, :], 0.0), axis=2)
    raised = jnp.exp(route_logits)
    route_weights = raised / jnp.sum(raised, axis=1, keepdims=True)
    weight_slots = jnp.sum(
        jnp.where(route_slots == slot_expert[:, None], route_weights, 0.0), axis=1
    )
    loss_slots = jnp.sum(jnp.where(pick, loss_weight[None, :], 0.0), axis=1)
    same = dot_last(pick_low, pick_low)
    grad_rows = (weight_slots * loss_slots)[:, None] * summed[:, :D]
    grad_rows = dot32(same, grad_rows, precision=HIGHEST)
    grad_share = loss_slots * share_slots
    token_share = jnp.sum(
        same[:, :, None] * (grad_share[:, None] * (slot_expert[:, None] == window))[None], axis=1
    )
    grad_weights = jnp.sum(
        jnp.where(route_slots[:, :, None] == window, token_share[:, None, :], 0.0), axis=2
    )
    grad_route = route_weights * (
        grad_weights - jnp.sum(route_weights * grad_weights, axis=1, keepdims=True)
    )
    grad_logits = jnp.sum(jnp.where(route_hot, grad_route[:, :, None], 0.0), axis=1).astype(BF16)
    grad_normed = dot_last(grad_logits, router) + grad_rows
    grad_unit = grad_normed * norm_gain[None, :]
    norm_grad = inv_rms * (
        grad_unit - unit_rows * jnp.mean(grad_unit * unit_rows, axis=1, keepdims=True)
    )
    earlier = jnp.tril(same, -1)
    primary = jnp.sum(earlier, axis=1) == 0
    place = jnp.where(primary[:, None], pick.astype(F32), 0.0)
    norm_part = lax.dot_general(
        place, norm_grad, (((0,), (0,)), ((), ())), precision=HIGHEST, preferred_element_type=F32
    )
    grad_residual = (loss_weight[:, None] * upstream[0].astype(F32) + norm_part).astype(BF16)

    grad_own = lax.dynamic_slice_in_dim(grad_residual, core * half, half, axis=1)
    grad_other = lax.dynamic_slice_in_dim(grad_residual, (1 - core) * half, half, axis=1)
    grad_attended = (dot_last(grad_own, own_out) + dot_last(grad_other, other_out)).astype(BF16)
    grad_q, grad_k, grad_v, grad_sinks = head_grads(
        probs, probs_low, sink_probs, query_rows, keys_here, values_here, grad_attended
    )
    sinks = jnp.pad(grad_sinks, (0, 128 - QUERY_HEADS))[None]
    sinks = jnp.sum(to_all(sinks, "dp"), axis=0)
    sinks = jnp.sum(to_all(sinks, "z"), axis=0)
    sinks = sinks + swap_cores(sinks)
    onward = jnp.concatenate([grad_k[:WINDOW], grad_v[:WINDOW]], axis=1).astype(BF16)
    onward = along_seq(onward, -1).astype(F32)
    grad_key_rows = (grad_k[WINDOW:] + onward[:, :kv_width]).astype(BF16)
    grad_value_rows = (grad_v[WINDOW:] + onward[:, kv_width:]).astype(BF16)
    return (
        grad_q[None],
        grad_key_rows[None],
        grad_value_rows[None],
        grad_residual[None],
        sinks[0, :QUERY_HEADS],
    )


def solution(mesh):
    seq, dp = mesh.shape["seq"], mesh.shape["dp"]
    split = Mesh(mesh.devices.reshape(seq // 2, 2, dp), ("z", "core", "dp"))
    whole = ("z", "core")
    return jax.shard_map(
        shards,
        mesh=split,
        in_specs=(
            P("dp", whole, None),
            P("dp", whole, None),
            P("dp", whole, None),
            P(),
            P("dp", whole, None),
            P("dp", None),
            P(),
            P(),
            P("dp", whole),
            P("dp", whole),
            P("dp", whole),
            P("dp", whole, None),
            P("dp"),
            P("dp"),
            P("dp", whole),
            P("dp", whole, None),
        ),
        out_specs=(
            P("dp", whole, None),
            P("dp", whole, None),
            P("dp", whole, None),
            P("dp", whole, None),
            P(),
        ),
        check_vma=False,
    )
```

```python
import jax
import jax.numpy as jnp
from jax import lax
from jax.sharding import Mesh, PartitionSpec as P

D = 2880
PADDED = 2944
HEAD_SIZE = 64
WINDOW = 128
EXPERTS = 128
QUERY_HEADS = 32
KEY_VALUE_HEADS = 4
EW = 2
CAP = 4
SLOTS = EW * CAP

NORM_EPS = 1e-05
GLU_SLOPE = 1.702
HIGHEST = lax.Precision.HIGHEST
CONTRACT_LAST = (((1,), (1,)), ((), ()))
F32 = jnp.float32
BF16 = jnp.bfloat16


def dot32(a, b, **kw):
    return jnp.dot(a, b, preferred_element_type=F32, **kw)


def dot_last(a, b):
    return lax.dot_general(a, b, CONTRACT_LAST, preferred_element_type=F32)


def exchange(value, axis):
    return lax.all_to_all(value, axis, split_axis=0, concat_axis=0, tiled=True)


def to_all(value, axis):
    count = lax.psum(1, axis)
    return exchange(jnp.broadcast_to(value[None], (count, *value.shape)), axis)


def swap_cores(value):
    return lax.ppermute(value, "core", [(0, 1), (1, 0)])


def along_seq(value, steps):
    chips, cores = lax.axis_size("z"), lax.axis_size("core")
    count = chips * cores
    first, last = max(0, -steps), min(count, count - steps)
    return lax.ppermute(value, ("z", "core"), [(i, i + steps) for i in range(first, last)])


def head_scores(query_rows, key_rows, sinks, allowed):
    tokens, keys = query_rows.shape[0], key_rows.shape[0]
    per_group = QUERY_HEADS // KEY_VALUE_HEADS
    q = query_rows.reshape(tokens, KEY_VALUE_HEADS, per_group, HEAD_SIZE)
    k = key_rows.reshape(keys, KEY_VALUE_HEADS, HEAD_SIZE)
    scores = jnp.einsum("baqj,eaj->aqbe", q, k, preferred_element_type=F32) * HEAD_SIZE**-0.5
    scores = jnp.where(allowed[None, None], scores, -1e30)
    sink_column = sinks.reshape(KEY_VALUE_HEADS, per_group)[:, :, None]
    largest = jnp.maximum(jnp.max(scores, axis=3), sink_column)
    raised = jnp.where(allowed[None, None], jnp.exp(scores - largest[..., None]), 0.0)
    sink_raised = jnp.exp(sink_column - largest)
    denominator = jnp.sum(raised, axis=3) + sink_raised
    return raised / denominator[..., None], sink_raised / denominator


def head_mix(probs_low, value_rows):
    v = value_rows.reshape(value_rows.shape[0], KEY_VALUE_HEADS, HEAD_SIZE)
    mixed = jnp.einsum("amlh,hai->lami", probs_low, v, preferred_element_type=F32)
    return mixed.reshape(mixed.shape[0], QUERY_HEADS * HEAD_SIZE).astype(BF16)


def head_grads(probs, probs_low, sink_probs, query_rows, key_rows, value_rows, grad_attended):
    tokens, keys = query_rows.shape[0], key_rows.shape[0]
    per_group = QUERY_HEADS // KEY_VALUE_HEADS
    q = query_rows.reshape(tokens, KEY_VALUE_HEADS, per_group, HEAD_SIZE)
    k = key_rows.reshape(keys, KEY_VALUE_HEADS, HEAD_SIZE)
    v = value_rows.reshape(keys, KEY_VALUE_HEADS, HEAD_SIZE)
    g = grad_attended.reshape(tokens, KEY_VALUE_HEADS, per_group, HEAD_SIZE)
    grad_prob = jnp.einsum("baqj,eaj->aqbe", g, v, preferred_element_type=F32)
    spread = jnp.sum(probs * grad_prob, axis=3)
    grad_score = (probs * (grad_prob - spread[..., None])).astype(BF16)
    scaling = HEAD_SIZE**-0.5
    grad_q = jnp.einsum("amlh,hai->lami", grad_score, k, preferred_element_type=F32) * scaling
    grad_k = jnp.einsum("ujko,kujm->oum", grad_score, q, preferred_element_type=F32) * scaling
    grad_v = jnp.einsum("ujko,kujm->oum", probs_low, g, preferred_element_type=F32)
    grad_sinks = -jnp.sum(sink_probs * spread, axis=2).reshape(QUERY_HEADS)
    return (
        grad_q.reshape(tokens, QUERY_HEADS * HEAD_SIZE).astype(BF16),
        grad_k.reshape(keys, KEY_VALUE_HEADS * HEAD_SIZE),
        grad_v.reshape(keys, KEY_VALUE_HEADS * HEAD_SIZE),
        grad_sinks,
    )


def shards(
    queries,
    key_rows,
    value_matrix,
    head_sink_logits,
    residual,
    out_weight,
    norm_gain,
    router,
    expert_gate,
    expert_up,
    expert_down,
    routes,
    group_ids,
    rewards,
    response_mask,
    upstream,
):
    chips, cores, dp_count = lax.axis_size("z"), lax.axis_size("core"), lax.axis_size("dp")
    seq_index = lax.axis_index("z") * cores + lax.axis_index("core")
    query_rows = queries[0]
    tokens = query_rows.shape[0]
    group_count = max(dp_count // 4, 1)
    all_tokens = dp_count * chips * cores * tokens
    lanes = out_weight.shape[0]

    route_rows = routes[0]
    window = jnp.arange(EW, dtype=jnp.int32)
    chosen = jnp.any(route_rows[:, :, None] == window, axis=1)
    below = jnp.arange(tokens)[:, None] >= jnp.arange(tokens)[None, :]
    rank = dot32(below.astype(BF16), chosen.astype(BF16)) - 1.0
    slot_hot = chosen.T[:, None, :] & (
        rank.T[:, None, :] == jnp.arange(CAP, dtype=F32)[None, :, None]
    )
    pick = slot_hot.reshape(SLOTS, tokens)
    pick_low = pick.astype(BF16)
    slot_expert = jnp.repeat(window, CAP)
    same = dot_last(pick_low, pick_low)
    primary = jnp.sum(jnp.tril(same, -1), axis=1) == 0
    place = jnp.where(primary[:, None], pick, False)
    taken = jnp.any(pick, axis=0)

    shard = jnp.stack([expert_gate, expert_up, expert_down])
    gathered = to_all(shard, "dp")
    out_full = lax.all_gather(out_weight, "dp", axis=0, tiled=True)
    hid = expert_gate.shape[1]

    halo = along_seq(jnp.concatenate([key_rows[0], value_matrix[0]], axis=1), 1)
    kv_width = key_rows.shape[2]
    keys_here = jnp.concatenate([halo[:, :kv_width], key_rows[0]], axis=0)
    values_here = jnp.concatenate([halo[:, kv_width:], value_matrix[0]], axis=0)
    row_index = jnp.arange(tokens, dtype=jnp.int32)[:, None]
    col_index = jnp.arange(WINDOW + tokens, dtype=jnp.int32)[None, :]

    def visible(rows):
        return (
            (col_index >= rows + 1)
            & (col_index <= rows + WINDOW)
            & ((col_index >= WINDOW) | (seq_index > 0))
        )

    slot_rows = jnp.sum(jnp.where(pick, row_index[:, 0][None, :], 0), axis=1, keepdims=True)
    query_slots = dot32(pick_low, query_rows).astype(BF16)
    probs_slots, sink_slots = head_scores(
        query_slots, keys_here, head_sink_logits, visible(slot_rows)
    )
    probs_slots_low = probs_slots.astype(BF16)
    attended_slots = head_mix(probs_slots_low, values_here)

    mask_wide = response_mask[0].astype(F32)
    facts = jnp.stack(
        [
            jnp.sum(mask_wide),
            rewards[0].astype(F32),
            group_ids[0].astype(F32),
        ]
    )
    facts_row = jnp.pad(facts, (0, lanes - 3))[None].astype(BF16)
    columns = attended_slots.reshape(SLOTS, dp_count, lanes).transpose(1, 0, 2)
    sent = jnp.concatenate(
        [columns, jnp.broadcast_to(facts_row[None], (dp_count, 1, lanes))], axis=1
    )
    sent = jnp.pad(sent, ((0, 0), (0, 2 * SLOTS - SLOTS - 1), (0, 0)))
    sent, gathered = lax.optimization_barrier((sent, gathered))
    arrived = exchange(sent, "dp")
    facts_all = arrived[:, SLOTS, :3].astype(F32)
    partial = dot32(arrived[:, :SLOTS].reshape(dp_count * SLOTS, lanes), out_weight)
    partial = exchange(partial.astype(BF16).reshape(dp_count, SLOTS, D), "dp")
    projected = jnp.sum(partial.astype(F32), axis=0)
    own_block = jnp.concatenate([gathered[:, i].reshape(D, -1) for i in range(3)], axis=1)
    other_block = swap_cores(own_block)

    residual_slots = dot32(pick_low, residual[0])
    upstream_slots = dot32(pick_low, upstream[0]).astype(BF16)
    mid = (residual_slots + projected).astype(BF16)
    mid_wide = lax.optimization_barrier(mid).astype(F32)
    inv_rms = lax.rsqrt(jnp.mean(mid_wide * mid_wide, axis=1, keepdims=True) + NORM_EPS)
    unit_rows = mid_wide * inv_rms
    normed = (unit_rows * norm_gain[None, :]).astype(BF16)

    counts_here = jnp.sum(facts_all[:, 0])
    group_hot = (facts_all[:, 2][:, None] == jnp.arange(group_count, dtype=F32)).astype(F32)
    reward_all = facts_all[:, 1]
    group_sizes = jnp.sum(group_hot, axis=0)
    group_sums = jnp.sum(group_hot * reward_all[:, None], axis=0)
    group_squares = jnp.sum(group_hot * (reward_all * reward_all)[:, None], axis=0)
    own_hot = group_ids[0] == jnp.arange(group_count, dtype=jnp.int32)
    means = group_sums / group_sizes
    spreads = group_squares / group_sizes - means * means
    own_mean = jnp.sum(jnp.where(own_hot, means, 0.0))
    own_spread = jnp.sum(jnp.where(own_hot, spreads, 0.0))
    advantage = (rewards[0].astype(F32) - own_mean) / jnp.sqrt(jnp.maximum(own_spread, 1.0))

    count_high = jnp.floor(counts_here / 64.0)
    count_tail = jnp.stack([count_high, counts_here - 64.0 * count_high])
    count_tail = jnp.pad(count_tail, (0, PADDED - D - 2)).astype(BF16)
    tails = jnp.broadcast_to(count_tail[None], (2 * SLOTS, PADDED - D))
    both = jnp.concatenate([jnp.concatenate([normed, upstream_slots], axis=0), tails], axis=1)
    at = jnp.arange(2 * SLOTS)
    source = (at // SLOTS) * CAP + at % CAP + jnp.where(at % SLOTS >= CAP, SLOTS, 0)
    arrange = (source[:, None] == at[None, :]).astype(BF16)
    by_expert = dot32(arrange, both).astype(BF16).reshape(EW, 1, 2 * CAP, PADDED)
    outgoing = jnp.broadcast_to(by_expert, (EW, chips // EW, 2 * CAP, PADDED))
    came = exchange(outgoing.reshape(chips, 2 * CAP, PADDED), "z")
    count_parts = jnp.sum(came[:, 0, D : D + 2].astype(F32), axis=0)
    core_count = count_parts[0] * 64.0 + count_parts[1]
    token_total = core_count + swap_cores(jnp.full((8, 128), core_count))[0, 0]
    token_scale = -advantage * all_tokens / token_total
    loss_weight = token_scale * mask_wide

    rows = came.reshape(chips * 2 * CAP, PADDED)[:, :D]
    shares = 0.0
    grads = []
    for block in (own_block, other_block):
        pre = dot32(rows, block).reshape(chips, 2 * CAP, 3 * hid)
        up_down = pre[:, CAP:, 2 * hid :].reshape(chips * CAP, hid)
        gate_pre = pre[:, :CAP, :hid].reshape(chips * CAP, hid)
        up_pre = pre[:, :CAP, hid : 2 * hid].reshape(chips * CAP, hid)
        sigmoid_gate = jax.nn.sigmoid(GLU_SLOPE * gate_pre)
        activation = ((up_pre + 1.0) * gate_pre * sigmoid_gate).astype(BF16)
        shares = shares + jnp.sum(activation.astype(F32) * up_down, axis=1)
        grad_up = up_down * (gate_pre * sigmoid_gate)
        grad_gate = (
            up_down
            * (up_pre + 1.0)
            * (sigmoid_gate + GLU_SLOPE * gate_pre * sigmoid_gate * (1.0 - sigmoid_gate))
        )
        grads.append(jnp.concatenate([grad_gate, grad_up], axis=1).astype(BF16))
    piece = dot_last(grads[0], own_block[:, : 2 * hid]) + dot_last(
        grads[1], other_block[:, : 2 * hid]
    )
    share_1 = shares.astype(BF16).astype(F32)
    share_2 = (shares - share_1).astype(BF16).astype(F32)
    share_3 = shares - share_1 - share_2
    tail = jnp.pad(jnp.stack([share_1, share_2, share_3], axis=1), ((0, 0), (0, PADDED - D - 3)))
    back = jnp.concatenate([piece, tail], axis=1).astype(BF16)
    back = exchange(back.reshape(chips, CAP, PADDED), "z")
    cot_rows = (loss_weight[:, None] * upstream[0].astype(F32)).astype(BF16)
    probs, sink_probs = head_scores(query_rows, keys_here, head_sink_logits, visible(row_index))
    grad_attended = jnp.where(taken[:, None], 0.0, dot_last(cot_rows, out_full)).astype(BF16)
    grad_q, grad_k, grad_v, grad_sinks = head_grads(
        probs, probs.astype(BF16), sink_probs, query_rows, keys_here, values_here, grad_attended
    )
    back, grad_q, grad_k, grad_v, grad_sinks = lax.optimization_barrier(
        (back, grad_q, grad_k, grad_v, grad_sinks)
    )
    summed = jnp.sum(back.reshape(EW, chips // EW, CAP, PADDED).astype(F32), axis=1)
    summed = summed.reshape(SLOTS, PADDED)
    share_slots = jnp.sum(summed[:, D : D + 3], axis=1)

    logits = dot32(normed, router)
    route_slots = dot32(pick_low, route_rows.astype(BF16)).astype(jnp.int32)
    route_hot = route_slots[:, :, None] == jnp.arange(EXPERTS, dtype=jnp.int32)
    route_logits = jnp.sum(jnp.where(route_hot, logits[:, None, :], 0.0), axis=2)
    raised = jnp.exp(route_logits)
    route_weights = raised / jnp.sum(raised, axis=1, keepdims=True)
    weight_slots = jnp.sum(
        jnp.where(route_slots == slot_expert[:, None], route_weights, 0.0), axis=1
    )
    loss_slots = jnp.sum(jnp.where(pick, loss_weight[None, :], 0.0), axis=1)
    cot_slots = loss_slots[:, None] * upstream_slots.astype(F32)
    grad_rows = (weight_slots * loss_slots)[:, None] * summed[:, :D]
    grad_rows = dot32(same, grad_rows, precision=HIGHEST)
    grad_share = loss_slots * share_slots
    token_share = jnp.sum(
        same[:, :, None] * (grad_share[:, None] * (slot_expert[:, None] == window))[None], axis=1
    )
    grad_weights = jnp.sum(
        jnp.where(route_slots[:, :, None] == window, token_share[:, None, :], 0.0), axis=2
    )
    grad_route = route_weights * (
        grad_weights - jnp.sum(route_weights * grad_weights, axis=1, keepdims=True)
    )
    grad_logits = jnp.sum(jnp.where(route_hot, grad_route[:, :, None], 0.0), axis=1).astype(BF16)
    grad_normed = dot_last(grad_logits, router) + grad_rows
    grad_unit = grad_normed * norm_gain[None, :]
    grad_slots = cot_slots + inv_rms * (
        grad_unit - unit_rows * jnp.mean(grad_unit * unit_rows, axis=1, keepdims=True)
    )
    grad_slots = jnp.where(primary[:, None], grad_slots, 0.0).astype(BF16)

    attended_grad_slots = dot_last(grad_slots, out_full).astype(BF16)
    slot_q, slot_k, slot_v, slot_sinks = head_grads(
        probs_slots,
        probs_slots_low,
        sink_slots,
        query_slots,
        keys_here,
        values_here,
        attended_grad_slots,
    )
    sinks = jnp.pad(grad_sinks + slot_sinks, (0, 128 - QUERY_HEADS))[None]
    sinks = jnp.sum(to_all(sinks, ("core", "dp")), axis=0)
    sinks = jnp.sum(to_all(sinks, "z"), axis=0)
    grad_k = grad_k + slot_k
    grad_v = grad_v + slot_v
    onward = jnp.concatenate([grad_k[:WINDOW], grad_v[:WINDOW]], axis=1).astype(BF16)
    onward = along_seq(onward, -1).astype(F32)
    grad_key_rows = (grad_k[WINDOW:] + onward[:, :kv_width]).astype(BF16)
    grad_value_rows = (grad_v[WINDOW:] + onward[:, kv_width:]).astype(BF16)
    put = place.astype(BF16)
    by_token = (((0,), (0,)), ((), ()))
    grad_residual = jnp.where(
        taken[:, None],
        lax.dot_general(put, grad_slots, by_token, preferred_element_type=F32).astype(BF16),
        cot_rows,
    )
    grad_q = jnp.where(
        taken[:, None],
        lax.dot_general(put, slot_q, by_token, preferred_element_type=F32).astype(BF16),
        grad_q,
    )
    return (
        grad_q[None],
        grad_key_rows[None],
        grad_value_rows[None],
        grad_residual[None],
        sinks[0, :QUERY_HEADS],
    )


def solution(mesh):
    seq, dp = mesh.shape["seq"], mesh.shape["dp"]
    split = Mesh(mesh.devices.reshape(seq // 2, 2, dp), ("z", "core", "dp"))
    whole = ("z", "core")
    return jax.shard_map(
        shards,
        mesh=split,
        in_specs=(
            P("dp", whole, None),
            P("dp", whole, None),
            P("dp", whole, None),
            P(),
            P("dp", whole, None),
            P("dp", None),
            P(),
            P(),
            P("dp", whole),
            P("dp", whole),
            P("dp", whole),
            P("dp", whole, None),
            P("dp"),
            P("dp"),
            P("dp", whole),
            P("dp", whole, None),
        ),
        out_specs=(
            P("dp", whole, None),
            P("dp", whole, None),
            P("dp", whole, None),
            P("dp", whole, None),
            P(),
        ),
        check_vma=False,
    )
```

```python
import jax
import jax.numpy as jnp
from jax import lax
from jax.sharding import Mesh, PartitionSpec as P

D = 2880
PADDED = 2944
HEAD_SIZE = 64
WINDOW = 128
EXPERTS = 128
QUERY_HEADS = 32
KEY_VALUE_HEADS = 4
EW = 2
CAP = 4
SLOTS = EW * CAP

NORM_EPS = 1e-05
GLU_SLOPE = 1.702
HIGHEST = lax.Precision.HIGHEST
CONTRACT_LAST = (((1,), (1,)), ((), ()))
F32 = jnp.float32
BF16 = jnp.bfloat16


def dot32(a, b, **kw):
    return jnp.dot(a, b, preferred_element_type=F32, **kw)


def dot_last(a, b):
    return lax.dot_general(a, b, CONTRACT_LAST, preferred_element_type=F32)


def exchange(value, axis):
    return lax.all_to_all(value, axis, split_axis=0, concat_axis=0, tiled=True)


def to_all(value, axis):
    count = lax.psum(1, axis)
    return exchange(jnp.broadcast_to(value[None], (count, *value.shape)), axis)


def swap_cores(value):
    return lax.ppermute(value, "core", [(0, 1), (1, 0)])


def along_seq(value, steps):
    chips, cores = lax.axis_size("z"), lax.axis_size("core")
    count = chips * cores
    first, last = max(0, -steps), min(count, count - steps)
    return lax.ppermute(value, ("z", "core"), [(i, i + steps) for i in range(first, last)])


def head_scores(query_rows, key_rows, sinks, allowed):
    tokens, keys = query_rows.shape[0], key_rows.shape[0]
    per_group = QUERY_HEADS // KEY_VALUE_HEADS
    q = query_rows.reshape(tokens, KEY_VALUE_HEADS, per_group, HEAD_SIZE)
    k = key_rows.reshape(keys, KEY_VALUE_HEADS, HEAD_SIZE)
    scores = jnp.einsum("baqj,eaj->aqbe", q, k, preferred_element_type=F32) * HEAD_SIZE**-0.5
    scores = jnp.where(allowed[None, None], scores, -1e30)
    sink_column = sinks.reshape(KEY_VALUE_HEADS, per_group)[:, :, None]
    largest = jnp.maximum(jnp.max(scores, axis=3), sink_column)
    raised = jnp.where(allowed[None, None], jnp.exp(scores - largest[..., None]), 0.0)
    sink_raised = jnp.exp(sink_column - largest)
    denominator = jnp.sum(raised, axis=3) + sink_raised
    return raised / denominator[..., None], sink_raised / denominator


def head_mix(probs_low, value_rows):
    v = value_rows.reshape(value_rows.shape[0], KEY_VALUE_HEADS, HEAD_SIZE)
    mixed = jnp.einsum("amlh,hai->lami", probs_low, v, preferred_element_type=F32)
    return mixed.reshape(mixed.shape[0], QUERY_HEADS * HEAD_SIZE).astype(BF16)


def head_grads(
    probs, probs_low, sink_probs, query_rows, key_rows, value_rows, grad_attended, scale
):
    tokens, keys = query_rows.shape[0], key_rows.shape[0]
    per_group = QUERY_HEADS // KEY_VALUE_HEADS
    q = query_rows.reshape(tokens, KEY_VALUE_HEADS, per_group, HEAD_SIZE)
    k = key_rows.reshape(keys, KEY_VALUE_HEADS, HEAD_SIZE)
    v = value_rows.reshape(keys, KEY_VALUE_HEADS, HEAD_SIZE)
    g = grad_attended.reshape(tokens, KEY_VALUE_HEADS, per_group, HEAD_SIZE)
    grad_prob = jnp.einsum("baqj,eaj->aqbe", g, v, preferred_element_type=F32)
    spread = jnp.sum(probs * grad_prob, axis=3)
    grad_score = (probs * (grad_prob - spread[..., None])).astype(BF16)
    scaling = HEAD_SIZE**-0.5 * scale
    grad_q = jnp.einsum("amlh,hai->lami", grad_score, k, preferred_element_type=F32) * scaling
    grad_k = jnp.einsum("ujko,kujm->oum", grad_score, q, preferred_element_type=F32) * scaling
    grad_v = jnp.einsum("ujko,kujm->oum", probs_low, g, preferred_element_type=F32) * scale
    grad_sinks = -jnp.sum(sink_probs * spread, axis=2).reshape(QUERY_HEADS) * scale
    return (
        grad_q.reshape(tokens, QUERY_HEADS * HEAD_SIZE).astype(BF16),
        grad_k.reshape(keys, KEY_VALUE_HEADS * HEAD_SIZE),
        grad_v.reshape(keys, KEY_VALUE_HEADS * HEAD_SIZE),
        grad_sinks,
    )


def shards(
    queries,
    key_rows,
    value_matrix,
    head_sink_logits,
    residual,
    out_weight,
    norm_gain,
    router,
    expert_gate,
    expert_up,
    expert_down,
    routes,
    group_ids,
    rewards,
    response_mask,
    upstream,
):
    chips, cores, dp_count = lax.axis_size("z"), lax.axis_size("core"), lax.axis_size("dp")
    seq_index = lax.axis_index("z") * cores + lax.axis_index("core")
    query_rows = queries[0]
    tokens = query_rows.shape[0]
    group_count = max(dp_count // 4, 1)
    all_tokens = dp_count * chips * cores * tokens
    lanes = out_weight.shape[0]

    route_rows = routes[0]
    window = jnp.arange(EW, dtype=jnp.int32)
    chosen = jnp.any(route_rows[:, :, None] == window, axis=1)
    below = jnp.arange(tokens)[:, None] >= jnp.arange(tokens)[None, :]
    rank = dot32(below.astype(BF16), chosen.astype(BF16)) - 1.0
    slot_hot = chosen.T[:, None, :] & (
        rank.T[:, None, :] == jnp.arange(CAP, dtype=F32)[None, :, None]
    )
    pick = slot_hot.reshape(SLOTS, tokens)
    pick_low = pick.astype(BF16)
    slot_expert = jnp.repeat(window, CAP)

    shard = jnp.stack([expert_gate, expert_up, expert_down])
    gathered = to_all(shard, "dp")
    hid = expert_gate.shape[1]

    halo = along_seq(jnp.concatenate([key_rows[0], value_matrix[0]], axis=1), 1)
    kv_width = key_rows.shape[2]
    keys_here = jnp.concatenate([halo[:, :kv_width], key_rows[0]], axis=0)
    values_here = jnp.concatenate([halo[:, kv_width:], value_matrix[0]], axis=0)
    row_index = jnp.arange(tokens, dtype=jnp.int32)[:, None]
    col_index = jnp.arange(WINDOW + tokens, dtype=jnp.int32)[None, :]

    def visible(rows):
        return (
            (col_index >= rows + 1)
            & (col_index <= rows + WINDOW)
            & ((col_index >= WINDOW) | (seq_index > 0))
        )

    slot_rows = jnp.sum(jnp.where(pick, row_index[:, 0][None, :], 0), axis=1, keepdims=True)
    query_slots = dot32(pick_low, query_rows).astype(BF16)
    probs_slots, sink_slots = head_scores(
        query_slots, keys_here, head_sink_logits, visible(slot_rows)
    )
    probs_slots_low = probs_slots.astype(BF16)
    attended_slots = head_mix(probs_slots_low, values_here)

    mask_wide = response_mask[0].astype(F32)
    facts = jnp.stack(
        [
            jnp.sum(mask_wide),
            rewards[0].astype(F32),
            group_ids[0].astype(F32),
        ]
    )
    facts_row = jnp.pad(facts, (0, lanes - 3))[None].astype(BF16)
    columns = attended_slots.reshape(SLOTS, dp_count, lanes).transpose(1, 0, 2)
    sent = jnp.concatenate(
        [columns, jnp.broadcast_to(facts_row[None], (dp_count, 1, lanes))], axis=1
    )
    sent = jnp.pad(sent, ((0, 0), (0, 2 * SLOTS - SLOTS - 1), (0, 0)))
    sent, gathered, late_weight = lax.optimization_barrier((sent, gathered, out_weight))
    out_full = lax.all_gather(late_weight, "dp", axis=0, tiled=True)
    arrived = exchange(sent, "dp")
    facts_all = arrived[:, SLOTS, :3].astype(F32)
    partial = dot32(arrived[:, :SLOTS].reshape(dp_count * SLOTS, lanes), out_weight)
    partial, residual_rows, upstream_rows, pick_low = lax.optimization_barrier(
        (partial.astype(BF16).reshape(dp_count, SLOTS, D), residual[0], upstream[0], pick_low)
    )
    partial = exchange(partial, "dp")
    pick = pick_low > 0
    projected = jnp.sum(partial.astype(F32), axis=0)
    own_block = jnp.concatenate([gathered[:, i].reshape(D, -1) for i in range(3)], axis=1)
    other_block = swap_cores(own_block)

    residual_slots = dot32(pick_low, residual_rows)
    upstream_slots = dot32(pick_low, upstream_rows).astype(BF16)
    mid = (residual_slots + projected).astype(BF16)
    mid_wide = lax.optimization_barrier(mid).astype(F32)
    inv_rms = lax.rsqrt(jnp.mean(mid_wide * mid_wide, axis=1, keepdims=True) + NORM_EPS)
    unit_rows = mid_wide * inv_rms
    normed = (unit_rows * norm_gain[None, :]).astype(BF16)

    counts_here = jnp.sum(facts_all[:, 0])
    group_hot = (facts_all[:, 2][:, None] == jnp.arange(group_count, dtype=F32)).astype(F32)
    reward_all = facts_all[:, 1]
    group_sizes = jnp.sum(group_hot, axis=0)
    group_sums = jnp.sum(group_hot * reward_all[:, None], axis=0)
    group_squares = jnp.sum(group_hot * (reward_all * reward_all)[:, None], axis=0)
    own_hot = group_ids[0] == jnp.arange(group_count, dtype=jnp.int32)
    means = group_sums / group_sizes
    spreads = group_squares / group_sizes - means * means
    own_mean = jnp.sum(jnp.where(own_hot, means, 0.0))
    own_spread = jnp.sum(jnp.where(own_hot, spreads, 0.0))
    advantage = (rewards[0].astype(F32) - own_mean) / jnp.sqrt(jnp.maximum(own_spread, 1.0))

    count_high = jnp.floor(counts_here / 64.0)
    count_tail = jnp.stack([count_high, counts_here - 64.0 * count_high])
    count_tail = jnp.pad(count_tail, (0, PADDED - D - 2)).astype(BF16)
    tails = jnp.broadcast_to(count_tail[None], (2 * SLOTS, PADDED - D))
    both = jnp.concatenate([jnp.concatenate([normed, upstream_slots], axis=0), tails], axis=1)
    at = jnp.arange(2 * SLOTS)
    source = (at // SLOTS) * CAP + at % CAP + jnp.where(at % SLOTS >= CAP, SLOTS, 0)
    arrange = (source[:, None] == at[None, :]).astype(BF16)
    by_expert = dot32(arrange, both).astype(BF16).reshape(EW, 1, 2 * CAP, PADDED)
    query_late, normed_late, route_late, upstream_rows, pick_low, by_expert = (
        lax.optimization_barrier(
            (query_rows, normed, route_rows, upstream_rows, pick_low, by_expert)
        )
    )
    pick = pick_low > 0
    same = dot_last(pick_low, pick_low)
    primary = jnp.sum(jnp.tril(same, -1), axis=1) == 0
    place = jnp.where(primary[:, None], pick, False)
    taken = jnp.any(pick, axis=0)
    outgoing = jnp.broadcast_to(by_expert, (EW, chips // EW, 2 * CAP, PADDED))
    came = exchange(outgoing.reshape(chips, 2 * CAP, PADDED), "z")

    rows = came.reshape(chips * 2 * CAP, PADDED)[:, :D]
    shares = 0.0
    grads = []
    for block in (own_block, other_block):
        pre = dot32(rows, block).reshape(chips, 2 * CAP, 3 * hid)
        up_down = pre[:, CAP:, 2 * hid :].reshape(chips * CAP, hid)
        gate_pre = pre[:, :CAP, :hid].reshape(chips * CAP, hid)
        up_pre = pre[:, :CAP, hid : 2 * hid].reshape(chips * CAP, hid)
        sigmoid_gate = jax.nn.sigmoid(GLU_SLOPE * gate_pre)
        activation = ((up_pre + 1.0) * gate_pre * sigmoid_gate).astype(BF16)
        shares = shares + jnp.sum(activation.astype(F32) * up_down, axis=1)
        grad_up = up_down * (gate_pre * sigmoid_gate)
        grad_gate = (
            up_down
            * (up_pre + 1.0)
            * (sigmoid_gate + GLU_SLOPE * gate_pre * sigmoid_gate * (1.0 - sigmoid_gate))
        )
        grads.append(jnp.concatenate([grad_gate, grad_up], axis=1).astype(BF16))
    piece = dot_last(grads[0], own_block[:, : 2 * hid]) + dot_last(
        grads[1], other_block[:, : 2 * hid]
    )
    share_1 = shares.astype(BF16).astype(F32)
    share_2 = (shares - share_1).astype(BF16).astype(F32)
    share_3 = shares - share_1 - share_2
    tail = jnp.pad(jnp.stack([share_1, share_2, share_3], axis=1), ((0, 0), (0, PADDED - D - 3)))
    back = jnp.concatenate([piece, tail], axis=1).astype(BF16)
    masked = jnp.where(mask_wide[:, None] > 0.0, upstream_rows, jnp.zeros_like(upstream_rows))
    back, masked = lax.optimization_barrier((back.reshape(chips, CAP, PADDED), masked))
    back = exchange(back, "z")

    grad_attended = jnp.where(taken[:, None], 0.0, dot_last(masked, out_full)).astype(BF16)
    came, grad_attended = lax.optimization_barrier((came, grad_attended))
    count_parts = jnp.sum(came[:, 0, D : D + 2].astype(F32), axis=0)
    core_count = count_parts[0] * 64.0 + count_parts[1]
    token_total = core_count + swap_cores(jnp.full((8, 128), core_count))[0, 0]
    token_scale = -advantage * all_tokens / token_total
    loss_weight = token_scale * mask_wide
    probs, sink_probs = head_scores(query_late, keys_here, head_sink_logits, visible(row_index))
    grad_q, grad_k, grad_v, grad_sinks = head_grads(
        probs,
        probs.astype(BF16),
        sink_probs,
        query_late,
        keys_here,
        values_here,
        grad_attended,
        token_scale,
    )
    back, grad_q, grad_k, grad_v, grad_sinks = lax.optimization_barrier(
        (back, grad_q, grad_k, grad_v, grad_sinks)
    )
    summed = jnp.sum(back.reshape(EW, chips // EW, CAP, PADDED).astype(F32), axis=1)
    summed = summed.reshape(SLOTS, PADDED)
    share_slots = jnp.sum(summed[:, D : D + 3], axis=1)

    logits = dot32(normed_late, router)
    route_slots = dot32(pick_low, route_late.astype(BF16)).astype(jnp.int32)
    route_hot = route_slots[:, :, None] == jnp.arange(EXPERTS, dtype=jnp.int32)
    route_logits = jnp.sum(jnp.where(route_hot, logits[:, None, :], 0.0), axis=2)
    raised = jnp.exp(route_logits)
    route_weights = raised / jnp.sum(raised, axis=1, keepdims=True)
    weight_slots = jnp.sum(
        jnp.where(route_slots == slot_expert[:, None], route_weights, 0.0), axis=1
    )
    loss_slots = jnp.sum(jnp.where(pick, loss_weight[None, :], 0.0), axis=1)
    cot_slots = loss_slots[:, None] * upstream_slots.astype(F32)
    grad_rows = (weight_slots * loss_slots)[:, None] * summed[:, :D]
    grad_rows = dot32(same, grad_rows, precision=HIGHEST)
    grad_share = loss_slots * share_slots
    token_share = jnp.sum(
        same[:, :, None] * (grad_share[:, None] * (slot_expert[:, None] == window))[None], axis=1
    )
    grad_weights = jnp.sum(
        jnp.where(route_slots[:, :, None] == window, token_share[:, None, :], 0.0), axis=2
    )
    grad_route = route_weights * (
        grad_weights - jnp.sum(route_weights * grad_weights, axis=1, keepdims=True)
    )
    grad_logits = jnp.sum(jnp.where(route_hot, grad_route[:, :, None], 0.0), axis=1).astype(BF16)
    grad_normed = dot_last(grad_logits, router) + grad_rows
    grad_unit = grad_normed * norm_gain[None, :]
    grad_slots = cot_slots + inv_rms * (
        grad_unit - unit_rows * jnp.mean(grad_unit * unit_rows, axis=1, keepdims=True)
    )
    grad_slots = jnp.where(primary[:, None], grad_slots, 0.0).astype(BF16)

    attended_grad_slots = dot_last(grad_slots, out_full).astype(BF16)
    slot_q, slot_k, slot_v, slot_sinks = head_grads(
        probs_slots,
        probs_slots_low,
        sink_slots,
        query_slots,
        keys_here,
        values_here,
        attended_grad_slots,
        1.0,
    )
    sinks = jnp.pad(grad_sinks + slot_sinks, (0, 128 - QUERY_HEADS))[None]
    sinks = jnp.sum(to_all(sinks, ("core", "dp")), axis=0)
    sinks = jnp.sum(to_all(sinks, "z"), axis=0)
    grad_k = grad_k + slot_k
    grad_v = grad_v + slot_v
    onward = jnp.concatenate([grad_k[:WINDOW], grad_v[:WINDOW]], axis=1).astype(BF16)
    onward = along_seq(onward, -1).astype(F32)
    grad_key_rows = (grad_k[WINDOW:] + onward[:, :kv_width]).astype(BF16)
    grad_value_rows = (grad_v[WINDOW:] + onward[:, kv_width:]).astype(BF16)
    cot_rows = (loss_weight[:, None] * upstream_rows.astype(F32)).astype(BF16)
    put = place.astype(BF16)
    by_token = (((0,), (0,)), ((), ()))
    grad_residual = jnp.where(
        taken[:, None],
        lax.dot_general(put, grad_slots, by_token, preferred_element_type=F32).astype(BF16),
        cot_rows,
    )
    grad_q = jnp.where(
        taken[:, None],
        lax.dot_general(put, slot_q, by_token, preferred_element_type=F32).astype(BF16),
        grad_q,
    )
    return (
        grad_q[None],
        grad_key_rows[None],
        grad_value_rows[None],
        grad_residual[None],
        sinks[0, :QUERY_HEADS],
    )


def solution(mesh):
    seq, dp = mesh.shape["seq"], mesh.shape["dp"]
    split = Mesh(mesh.devices.reshape(seq // 2, 2, dp), ("z", "core", "dp"))
    whole = ("z", "core")
    return jax.shard_map(
        shards,
        mesh=split,
        in_specs=(
            P("dp", whole, None),
            P("dp", whole, None),
            P("dp", whole, None),
            P(),
            P("dp", whole, None),
            P("dp", None),
            P(),
            P(),
            P("dp", whole),
            P("dp", whole),
            P("dp", whole),
            P("dp", whole, None),
            P("dp"),
            P("dp"),
            P("dp", whole),
            P("dp", whole, None),
        ),
        out_specs=(
            P("dp", whole, None),
            P("dp", whole, None),
            P("dp", whole, None),
            P("dp", whole, None),
            P(),
        ),
        check_vma=False,
    )
```

```python
import jax
import jax.numpy as jnp
from jax import lax
from jax.experimental import pallas as pl
from jax.experimental.pallas import tpu as pltpu
from jax.sharding import Mesh, PartitionSpec as P

D = 2880
PADDED = 2944
HEAD_SIZE = 64
WINDOW = 128
EXPERTS = 128
QUERY_HEADS = 32
KEY_VALUE_HEADS = 4
EW = 2
CAP = 4
SLOTS = EW * CAP

NORM_EPS = 1e-05
GLU_SLOPE = 1.702
HIGHEST = lax.Precision.HIGHEST
CONTRACT_LAST = (((1,), (1,)), ((), ()))
F32 = jnp.float32
BF16 = jnp.bfloat16


def dot32(a, b, **kw):
    return jnp.dot(a, b, preferred_element_type=F32, **kw)


def dot_last(a, b):
    return lax.dot_general(a, b, CONTRACT_LAST, preferred_element_type=F32)


def exchange(value, axis):
    return lax.all_to_all(value, axis, split_axis=0, concat_axis=0, tiled=True)


def to_all(value, axis):
    count = lax.psum(1, axis)
    return exchange(jnp.broadcast_to(value[None], (count, *value.shape)), axis)


def swap_cores(value):
    return lax.ppermute(value, "core", [(0, 1), (1, 0)])


def along_seq(value, steps):
    chips, cores = lax.axis_size("z"), lax.axis_size("core")
    count = chips * cores
    first, last = max(0, -steps), min(count, count - steps)
    return lax.ppermute(value, ("z", "core"), [(i, i + steps) for i in range(first, last)])


def head_scores(query_rows, key_rows, sinks, allowed):
    tokens, keys = query_rows.shape[0], key_rows.shape[0]
    per_group = QUERY_HEADS // KEY_VALUE_HEADS
    q = query_rows.reshape(tokens, KEY_VALUE_HEADS, per_group, HEAD_SIZE)
    k = key_rows.reshape(keys, KEY_VALUE_HEADS, HEAD_SIZE)
    scores = jnp.einsum("baqj,eaj->aqbe", q, k, preferred_element_type=F32) * HEAD_SIZE**-0.5
    scores = jnp.where(allowed[None, None], scores, -1e30)
    sink_column = sinks.reshape(KEY_VALUE_HEADS, per_group)[:, :, None]
    largest = jnp.maximum(jnp.max(scores, axis=3), sink_column)
    raised = jnp.where(allowed[None, None], jnp.exp(scores - largest[..., None]), 0.0)
    sink_raised = jnp.exp(sink_column - largest)
    denominator = jnp.sum(raised, axis=3) + sink_raised
    return raised / denominator[..., None], sink_raised / denominator


def head_mix(probs_low, value_rows):
    v = value_rows.reshape(value_rows.shape[0], KEY_VALUE_HEADS, HEAD_SIZE)
    mixed = jnp.einsum("amlh,hai->lami", probs_low, v, preferred_element_type=F32)
    return mixed.reshape(mixed.shape[0], QUERY_HEADS * HEAD_SIZE).astype(BF16)


def head_spread(probs, value_rows, grad_attended):
    tokens, keys = grad_attended.shape[0], value_rows.shape[0]
    per_group = QUERY_HEADS // KEY_VALUE_HEADS
    v = value_rows.reshape(keys, KEY_VALUE_HEADS, HEAD_SIZE)
    g = grad_attended.reshape(tokens, KEY_VALUE_HEADS, per_group, HEAD_SIZE)
    grad_prob = jnp.einsum("baqj,eaj->aqbe", g, v, preferred_element_type=F32)
    return grad_prob, jnp.sum(probs * grad_prob, axis=3)


def head_grads(probs, grad_prob, spread, query_rows, key_rows, grad_attended, scale):
    tokens, keys = query_rows.shape[0], key_rows.shape[0]
    per_group = QUERY_HEADS // KEY_VALUE_HEADS
    q = query_rows.reshape(tokens, KEY_VALUE_HEADS, per_group, HEAD_SIZE)
    k = key_rows.reshape(keys, KEY_VALUE_HEADS, HEAD_SIZE)
    g = grad_attended.reshape(tokens, KEY_VALUE_HEADS, per_group, HEAD_SIZE)
    grad_score = (probs * (grad_prob - spread[..., None])).astype(BF16)
    probs_low = probs.astype(BF16)
    scaling = HEAD_SIZE**-0.5 * scale
    grad_q = jnp.einsum("amlh,hai->lami", grad_score, k, preferred_element_type=F32) * scaling
    grad_k = jnp.einsum("ujko,kujm->oum", grad_score, q, preferred_element_type=F32) * scaling
    grad_v = jnp.einsum("ujko,kujm->oum", probs_low, g, preferred_element_type=F32) * scale
    return (
        grad_q.reshape(tokens, QUERY_HEADS * HEAD_SIZE).astype(BF16),
        grad_k.reshape(keys, KEY_VALUE_HEADS * HEAD_SIZE),
        grad_v.reshape(keys, KEY_VALUE_HEADS * HEAD_SIZE),
    )


def experts_kernel(rows_ref, own_ref, other_ref, out_ref):
    count = rows_ref.shape[0]
    kept = count // 2
    hid = own_ref.shape[1] // 3
    at = lax.broadcasted_iota(jnp.int32, (kept, count), 0)
    source = (at // CAP) * (2 * CAP) + at % CAP
    column = lax.broadcasted_iota(jnp.int32, (kept, count), 1)
    rows = rows_ref[:, :D]
    normed = dot32((column == source).astype(BF16), rows).astype(BF16)
    upstream = dot32((column == source + CAP).astype(BF16), rows).astype(BF16)
    piece = jnp.zeros((kept, D), F32)
    share = jnp.zeros((kept, 1), F32)
    for block in (own_ref, other_ref):
        pair = block[:, : 2 * hid]
        pre = dot32(normed, pair)
        up_down = dot32(upstream, block[:, 2 * hid :])
        gate_pre, up_pre = pre[:, :hid], pre[:, hid:]
        sigmoid_gate = jax.nn.sigmoid(GLU_SLOPE * gate_pre)
        activation = ((up_pre + 1.0) * gate_pre * sigmoid_gate).astype(BF16)
        share = share + jnp.sum(activation.astype(F32) * up_down, axis=1, keepdims=True)
        grad_up = up_down * (gate_pre * sigmoid_gate)
        grad_gate = (
            up_down
            * (up_pre + 1.0)
            * (sigmoid_gate + GLU_SLOPE * gate_pre * sigmoid_gate * (1.0 - sigmoid_gate))
        )
        grads = jnp.concatenate([grad_gate, grad_up], axis=1).astype(BF16)
        piece = piece + dot_last(grads, pair)
    share_1 = share.astype(BF16).astype(F32)
    share_2 = (share - share_1).astype(BF16).astype(F32)
    share_3 = share - share_1 - share_2
    lane = lax.broadcasted_iota(jnp.int32, (kept, PADDED - D), 1)
    tail = jnp.where(lane == 0, share_1, jnp.where(lane == 1, share_2, 0.0))
    tail = jnp.where(lane == 2, share_3, tail)
    even = (D // 128) * 128
    out_ref[:, :even] = piece[:, :even].astype(BF16)
    out_ref[:, even:] = jnp.concatenate([piece[:, even:], tail], axis=1).astype(BF16)


def experts_step(rows, own_block, other_block):
    count, hid = rows.shape[0], own_block.shape[1] // 3
    return pl.pallas_call(
        experts_kernel,
        out_shape=jax.ShapeDtypeStruct((count // 2, PADDED), BF16),
        in_specs=[pl.BlockSpec(memory_space=pltpu.VMEM)] * 3,
        out_specs=pl.BlockSpec(memory_space=pltpu.VMEM),
        compiler_params=pltpu.CompilerParams(vmem_limit_bytes=24 << 20),
        cost_estimate=pl.CostEstimate(
            flops=2 * 2 * count // 2 * D * hid * 5,
            bytes_accessed=2 * (2 * D * 3 * hid + 2 * count * PADDED),
            transcendentals=count * hid,
        ),
    )(rows, own_block, other_block)


def shards(
    queries,
    key_rows,
    value_matrix,
    head_sink_logits,
    residual,
    out_weight,
    norm_gain,
    router,
    expert_gate,
    expert_up,
    expert_down,
    routes,
    group_ids,
    rewards,
    response_mask,
    upstream,
):
    chips, cores, dp_count = lax.axis_size("z"), lax.axis_size("core"), lax.axis_size("dp")
    seq_index = lax.axis_index("z") * cores + lax.axis_index("core")
    query_rows = queries[0]
    tokens = query_rows.shape[0]
    group_count = max(dp_count // 4, 1)
    all_tokens = dp_count * chips * cores * tokens
    lanes = out_weight.shape[0]

    route_rows = routes[0]
    window = jnp.arange(EW, dtype=jnp.int32)
    chosen = jnp.any(route_rows[:, :, None] == window, axis=1)
    below = jnp.arange(tokens)[:, None] >= jnp.arange(tokens)[None, :]
    rank = dot32(below.astype(BF16), chosen.astype(BF16)) - 1.0
    slot_hot = chosen.T[:, None, :] & (
        rank.T[:, None, :] == jnp.arange(CAP, dtype=F32)[None, :, None]
    )
    pick = slot_hot.reshape(SLOTS, tokens)
    pick_low = pick.astype(BF16)
    slot_expert = jnp.repeat(window, CAP)

    shard = jnp.concatenate([expert_gate, expert_up, expert_down], axis=1)
    spread_shard = jnp.broadcast_to(shard[None], (dp_count, *shard.shape))
    spread_shard, own_keys, own_values = lax.optimization_barrier(
        (spread_shard, key_rows[0], value_matrix[0])
    )
    gathered = exchange(spread_shard, "dp")

    halo = along_seq(jnp.concatenate([own_keys, own_values], axis=1), 1)
    kv_width = key_rows.shape[2]
    keys_here = jnp.concatenate([halo[:, :kv_width], own_keys], axis=0)
    values_here = jnp.concatenate([halo[:, kv_width:], own_values], axis=0)
    row_index = jnp.arange(tokens, dtype=jnp.int32)[:, None]
    col_index = jnp.arange(WINDOW + tokens, dtype=jnp.int32)[None, :]

    def visible(rows, columns):
        return (
            (columns >= rows + 1)
            & (columns <= rows + WINDOW)
            & ((columns >= WINDOW) | (seq_index > 0))
        )

    slot_rows = jnp.sum(jnp.where(pick, row_index[:, 0][None, :], 0), axis=1, keepdims=True)
    query_slots = dot32(pick_low, query_rows).astype(BF16)
    probs_slots, sink_slots = head_scores(
        query_slots, keys_here, head_sink_logits, visible(slot_rows, col_index)
    )
    attended_slots = head_mix(probs_slots.astype(BF16), values_here)

    mask_wide = response_mask[0].astype(F32)
    facts = jnp.stack(
        [
            jnp.sum(mask_wide),
            rewards[0].astype(F32),
            group_ids[0].astype(F32),
        ]
    )
    facts_row = jnp.pad(facts, (0, lanes - 3))[None].astype(BF16)
    columns = attended_slots.reshape(SLOTS, dp_count, lanes).transpose(1, 0, 2)
    sent = jnp.concatenate(
        [columns, jnp.broadcast_to(facts_row[None], (dp_count, 1, lanes))], axis=1
    )
    sent = jnp.pad(sent, ((0, 0), (0, 2 * SLOTS - SLOTS - 1), (0, 0)))
    sent, gathered, late_weight = lax.optimization_barrier((sent, gathered, out_weight))
    out_full = lax.all_gather(late_weight, "dp", axis=0, tiled=True)
    arrived = exchange(sent, "dp")
    facts_all = arrived[:, SLOTS, :3].astype(F32)
    partial = dot32(arrived[:, :SLOTS].reshape(dp_count * SLOTS, lanes), out_weight)
    partial, residual_rows, upstream_rows, pick_low = lax.optimization_barrier(
        (partial.astype(BF16).reshape(dp_count, SLOTS, D), residual[0], upstream[0], pick_low)
    )
    partial = exchange(partial, "dp")
    pick = pick_low > 0
    projected = jnp.sum(partial.astype(F32), axis=0)
    own_block = gathered.reshape(D, shard.shape[1])
    other_block = swap_cores(own_block)

    residual_slots = dot32(pick_low, residual_rows)
    upstream_slots = dot32(pick_low, upstream_rows).astype(BF16)
    mid = (residual_slots + projected).astype(BF16)
    mid_wide = lax.optimization_barrier(mid).astype(F32)
    inv_rms = lax.rsqrt(jnp.mean(mid_wide * mid_wide, axis=1, keepdims=True) + NORM_EPS)
    unit_rows = mid_wide * inv_rms
    normed = (unit_rows * norm_gain[None, :]).astype(BF16)

    counts_here = jnp.sum(facts_all[:, 0])
    group_hot = (facts_all[:, 2][:, None] == jnp.arange(group_count, dtype=F32)).astype(F32)
    reward_all = facts_all[:, 1]
    group_sizes = jnp.sum(group_hot, axis=0)
    group_sums = jnp.sum(group_hot * reward_all[:, None], axis=0)
    group_squares = jnp.sum(group_hot * (reward_all * reward_all)[:, None], axis=0)
    own_hot = group_ids[0] == jnp.arange(group_count, dtype=jnp.int32)
    means = group_sums / group_sizes
    spreads = group_squares / group_sizes - means * means
    own_mean = jnp.sum(jnp.where(own_hot, means, 0.0))
    own_spread = jnp.sum(jnp.where(own_hot, spreads, 0.0))
    advantage = (rewards[0].astype(F32) - own_mean) / jnp.sqrt(jnp.maximum(own_spread, 1.0))

    count_high = jnp.floor(counts_here / 64.0)
    count_tail = jnp.stack([count_high, counts_here - 64.0 * count_high])
    count_tail = jnp.pad(count_tail, (0, PADDED - D - 2)).astype(BF16)
    tails = jnp.broadcast_to(count_tail[None], (2 * SLOTS, PADDED - D))
    both = jnp.concatenate([jnp.concatenate([normed, upstream_slots], axis=0), tails], axis=1)
    at = jnp.arange(2 * SLOTS)
    source = (at // SLOTS) * CAP + at % CAP + jnp.where(at % SLOTS >= CAP, SLOTS, 0)
    arrange = (source[:, None] == at[None, :]).astype(BF16)
    by_expert = dot32(arrange, both).astype(BF16).reshape(EW, 1, 2 * CAP, PADDED)
    query_late, normed_late, route_late, upstream_rows, pick_low, by_expert, row_late, col_late = (
        lax.optimization_barrier(
            (
                query_rows,
                normed,
                route_rows,
                upstream_rows,
                pick_low,
                by_expert,
                row_index,
                col_index,
            )
        )
    )
    pick = pick_low > 0
    same = dot_last(pick_low, pick_low)
    primary = jnp.sum(jnp.tril(same, -1), axis=1) == 0
    place = jnp.where(primary[:, None], pick, False)
    taken = jnp.any(pick, axis=0)
    outgoing = jnp.broadcast_to(by_expert, (EW, chips // EW, 2 * CAP, PADDED))
    came = exchange(outgoing.reshape(chips, 2 * CAP, PADDED), "z")

    back = experts_step(came.reshape(chips * 2 * CAP, PADDED), own_block, other_block)
    back, mask_late = lax.optimization_barrier((back.reshape(chips, CAP, PADDED), mask_wide))
    back = exchange(back, "z")

    masked = jnp.where(mask_late[:, None] > 0.0, upstream_rows, jnp.zeros_like(upstream_rows))
    grad_attended = jnp.where(taken[:, None], 0.0, dot_last(masked, out_full)).astype(BF16)
    came, grad_attended = lax.optimization_barrier((came, grad_attended))
    count_parts = jnp.sum(came[:, 0, D : D + 2].astype(F32), axis=0)
    core_count = count_parts[0] * 64.0 + count_parts[1]
    token_total = core_count + swap_cores(jnp.full((8, 128), core_count))[0, 0]
    token_scale = -advantage * all_tokens / token_total
    loss_weight = token_scale * mask_late
    probs, sink_probs = head_scores(
        query_late, keys_here, head_sink_logits, visible(row_late, col_late)
    )
    grad_prob, spread = head_spread(probs, values_here, grad_attended)
    grad_q, grad_k, grad_v = head_grads(
        probs, grad_prob, spread, query_late, keys_here, grad_attended, token_scale
    )
    back, grad_q, grad_k, grad_v, spread = lax.optimization_barrier(
        (back, grad_q, grad_k, grad_v, spread)
    )
    dense_sinks = jnp.sum(sink_probs * spread, axis=2).reshape(QUERY_HEADS) * token_scale
    summed = jnp.sum(back.reshape(EW, chips // EW, CAP, PADDED).astype(F32), axis=1)
    summed = summed.reshape(SLOTS, PADDED)
    share_slots = jnp.sum(summed[:, D : D + 3], axis=1)

    logits = dot32(normed_late, router)
    route_slots = dot32(pick_low, route_late.astype(BF16)).astype(jnp.int32)
    route_hot = route_slots[:, :, None] == jnp.arange(EXPERTS, dtype=jnp.int32)
    route_logits = jnp.sum(jnp.where(route_hot, logits[:, None, :], 0.0), axis=2)
    raised = jnp.exp(route_logits)
    route_weights = raised / jnp.sum(raised, axis=1, keepdims=True)
    weight_slots = jnp.sum(
        jnp.where(route_slots == slot_expert[:, None], route_weights, 0.0), axis=1
    )
    loss_slots = jnp.sum(jnp.where(pick, loss_weight[None, :], 0.0), axis=1)
    cot_slots = loss_slots[:, None] * upstream_slots.astype(F32)
    grad_rows = (weight_slots * loss_slots)[:, None] * summed[:, :D]
    grad_rows = dot32(same, grad_rows, precision=HIGHEST)
    grad_share = loss_slots * share_slots
    token_share = jnp.sum(
        same[:, :, None] * (grad_share[:, None] * (slot_expert[:, None] == window))[None], axis=1
    )
    grad_weights = jnp.sum(
        jnp.where(route_slots[:, :, None] == window, token_share[:, None, :], 0.0), axis=2
    )
    grad_route = route_weights * (
        grad_weights - jnp.sum(route_weights * grad_weights, axis=1, keepdims=True)
    )
    grad_logits = jnp.sum(jnp.where(route_hot, grad_route[:, :, None], 0.0), axis=1).astype(BF16)
    grad_normed = dot_last(grad_logits, router) + grad_rows
    grad_unit = grad_normed * norm_gain[None, :]
    grad_slots = cot_slots + inv_rms * (
        grad_unit - unit_rows * jnp.mean(grad_unit * unit_rows, axis=1, keepdims=True)
    )
    grad_slots = jnp.where(primary[:, None], grad_slots, 0.0).astype(BF16)

    attended_grad_slots = dot_last(grad_slots, out_full).astype(BF16)
    slot_prob, slot_spread = head_spread(probs_slots, values_here, attended_grad_slots)
    slot_sinks = jnp.sum(sink_slots * slot_spread, axis=2).reshape(QUERY_HEADS)
    sinks = jnp.pad(-(dense_sinks + slot_sinks), (0, 128 - QUERY_HEADS))[None]
    sinks = to_all(sinks, ("core", "dp"))
    sinks, slot_prob, upstream_rows = lax.optimization_barrier(
        (jnp.sum(sinks, axis=0), slot_prob, upstream_rows)
    )
    sinks = to_all(sinks, "z")
    sinks = jnp.sum(sinks, axis=0)

    slot_q, slot_k, slot_v = head_grads(
        probs_slots, slot_prob, slot_spread, query_slots, keys_here, attended_grad_slots, 1.0
    )
    grad_k = grad_k + slot_k
    grad_v = grad_v + slot_v
    onward = jnp.concatenate([grad_k[:WINDOW], grad_v[:WINDOW]], axis=1).astype(BF16)
    onward = along_seq(onward, -1).astype(F32)
    grad_key_rows = (grad_k[WINDOW:] + onward[:, :kv_width]).astype(BF16)
    grad_value_rows = (grad_v[WINDOW:] + onward[:, kv_width:]).astype(BF16)
    cot_rows = (loss_weight[:, None] * upstream_rows.astype(F32)).astype(BF16)
    put = place.astype(BF16)
    by_token = (((0,), (0,)), ((), ()))
    grad_residual = jnp.where(
        taken[:, None],
        lax.dot_general(put, grad_slots, by_token, preferred_element_type=F32).astype(BF16),
        cot_rows,
    )
    grad_q = jnp.where(
        taken[:, None],
        lax.dot_general(put, slot_q, by_token, preferred_element_type=F32).astype(BF16),
        grad_q,
    )
    return (
        grad_q[None],
        grad_key_rows[None],
        grad_value_rows[None],
        grad_residual[None],
        sinks[0, :QUERY_HEADS],
    )


def solution(mesh):
    seq, dp = mesh.shape["seq"], mesh.shape["dp"]
    split = Mesh(mesh.devices.reshape(seq // 2, 2, dp), ("z", "core", "dp"))
    whole = ("z", "core")

    return jax.shard_map(
        shards,
        mesh=split,
        in_specs=(
            P("dp", whole, None),
            P("dp", whole, None),
            P("dp", whole, None),
            P(),
            P("dp", whole, None),
            P("dp", None),
            P(),
            P(),
            P("dp", whole),
            P("dp", whole),
            P("dp", whole),
            P("dp", whole, None),
            P("dp"),
            P("dp"),
            P("dp", whole),
            P("dp", whole, None),
        ),
        out_specs=(
            P("dp", whole, None),
            P("dp", whole, None),
            P("dp", whole, None),
            P("dp", whole, None),
            P(),
        ),
        check_vma=False,
    )
```

```python
import jax
import jax.numpy as jnp
from jax import lax
from jax.experimental import pallas as pl
from jax.experimental.pallas import tpu as pltpu
from jax.sharding import Mesh, PartitionSpec as P

D = 2880
PADDED = 2944
HEAD_SIZE = 64
WINDOW = 128
EXPERTS = 128
QUERY_HEADS = 32
KEY_VALUE_HEADS = 4
EW = 2
CAP = 4
SLOTS = EW * CAP

NORM_EPS = 1e-05
GLU_SLOPE = 1.702
HIGHEST = lax.Precision.HIGHEST
SEQ = ("pair", "half", "core")
CONTRACT_LAST = (((1,), (1,)), ((), ()))
F32 = jnp.float32
BF16 = jnp.bfloat16


def dot32(a, b, **kw):
    return jnp.dot(a, b, preferred_element_type=F32, **kw)


def dot_last(a, b):
    return lax.dot_general(a, b, CONTRACT_LAST, preferred_element_type=F32)


def exchange(value, axis):
    return lax.all_to_all(value, axis, split_axis=0, concat_axis=0, tiled=True)


def to_all(value, axis):
    count = lax.psum(1, axis)
    return exchange(jnp.broadcast_to(value[None], (count, *value.shape)), axis)


def swap(value, axis):
    return lax.ppermute(value, axis, [(0, 1), (1, 0)])


def along_seq(value, steps):
    count = lax.psum(1, SEQ)
    first, last = max(0, -steps), min(count, count - steps)
    return lax.ppermute(value, SEQ, [(i, i + steps) for i in range(first, last)])


def head_scores(query_rows, key_rows, sinks, allowed):
    tokens, keys = query_rows.shape[0], key_rows.shape[0]
    per_group = QUERY_HEADS // KEY_VALUE_HEADS
    q = query_rows.reshape(tokens, KEY_VALUE_HEADS, per_group, HEAD_SIZE)
    k = key_rows.reshape(keys, KEY_VALUE_HEADS, HEAD_SIZE)
    scores = jnp.einsum("baqj,eaj->aqbe", q, k, preferred_element_type=F32) * HEAD_SIZE**-0.5
    scores = jnp.where(allowed[None, None], scores, -1e30)
    sink_column = sinks.reshape(KEY_VALUE_HEADS, per_group)[:, :, None]
    largest = jnp.maximum(jnp.max(scores, axis=3), sink_column)
    raised = jnp.where(allowed[None, None], jnp.exp(scores - largest[..., None]), 0.0)
    sink_raised = jnp.exp(sink_column - largest)
    denominator = jnp.sum(raised, axis=3) + sink_raised
    return raised / denominator[..., None], sink_raised / denominator


def head_mix(probs_low, value_rows):
    v = value_rows.reshape(value_rows.shape[0], KEY_VALUE_HEADS, HEAD_SIZE)
    mixed = jnp.einsum("amlh,hai->lami", probs_low, v, preferred_element_type=F32)
    return mixed.reshape(mixed.shape[0], QUERY_HEADS * HEAD_SIZE).astype(BF16)


def head_spread(probs, value_rows, grad_attended):
    tokens, keys = grad_attended.shape[0], value_rows.shape[0]
    per_group = QUERY_HEADS // KEY_VALUE_HEADS
    v = value_rows.reshape(keys, KEY_VALUE_HEADS, HEAD_SIZE)
    g = grad_attended.reshape(tokens, KEY_VALUE_HEADS, per_group, HEAD_SIZE)
    grad_prob = jnp.einsum("baqj,eaj->aqbe", g, v, preferred_element_type=F32)
    return grad_prob, jnp.sum(probs * grad_prob, axis=3)


def head_grads(probs, grad_prob, spread, query_rows, key_rows, grad_attended, scale):
    tokens, keys = query_rows.shape[0], key_rows.shape[0]
    per_group = QUERY_HEADS // KEY_VALUE_HEADS
    q = query_rows.reshape(tokens, KEY_VALUE_HEADS, per_group, HEAD_SIZE)
    k = key_rows.reshape(keys, KEY_VALUE_HEADS, HEAD_SIZE)
    g = grad_attended.reshape(tokens, KEY_VALUE_HEADS, per_group, HEAD_SIZE)
    grad_score = (probs * (grad_prob - spread[..., None])).astype(BF16)
    probs_low = probs.astype(BF16)
    scaling = HEAD_SIZE**-0.5 * scale
    grad_q = jnp.einsum("amlh,hai->lami", grad_score, k, preferred_element_type=F32) * scaling
    grad_k = jnp.einsum("ujko,kujm->oum", grad_score, q, preferred_element_type=F32) * scaling
    grad_v = jnp.einsum("ujko,kujm->oum", probs_low, g, preferred_element_type=F32) * scale
    return (
        grad_q.reshape(tokens, QUERY_HEADS * HEAD_SIZE).astype(BF16),
        grad_k.reshape(keys, KEY_VALUE_HEADS * HEAD_SIZE),
        grad_v.reshape(keys, KEY_VALUE_HEADS * HEAD_SIZE),
    )


def experts_kernel(rows_ref, *refs):
    blocks, out_ref = refs[:-1], refs[-1]
    count = rows_ref.shape[0]
    kept = count // 2
    hid = blocks[0].shape[1] // 3
    at = lax.broadcasted_iota(jnp.int32, (kept, count), 0)
    source = (at // CAP) * (2 * CAP) + at % CAP
    column = lax.broadcasted_iota(jnp.int32, (kept, count), 1)
    rows = rows_ref[:, :D]
    normed = dot32((column == source).astype(BF16), rows).astype(BF16)
    upstream = dot32((column == source + CAP).astype(BF16), rows).astype(BF16)
    piece = jnp.zeros((kept, D), F32)
    share = jnp.zeros((kept, 1), F32)
    for block in blocks:
        pair = block[:, : 2 * hid]
        pre = dot32(normed, pair)
        up_down = dot32(upstream, block[:, 2 * hid :])
        gate_pre, up_pre = pre[:, :hid], pre[:, hid:]
        sigmoid_gate = jax.nn.sigmoid(GLU_SLOPE * gate_pre)
        activation = ((up_pre + 1.0) * gate_pre * sigmoid_gate).astype(BF16)
        share = share + jnp.sum(activation.astype(F32) * up_down, axis=1, keepdims=True)
        grad_up = up_down * (gate_pre * sigmoid_gate)
        grad_gate = (
            up_down
            * (up_pre + 1.0)
            * (sigmoid_gate + GLU_SLOPE * gate_pre * sigmoid_gate * (1.0 - sigmoid_gate))
        )
        grads = jnp.concatenate([grad_gate, grad_up], axis=1).astype(BF16)
        piece = piece + dot_last(grads, pair)
    share_1 = share.astype(BF16).astype(F32)
    share_2 = (share - share_1).astype(BF16).astype(F32)
    share_3 = share - share_1 - share_2
    lane = lax.broadcasted_iota(jnp.int32, (kept, PADDED - D), 1)
    tail = jnp.where(lane == 0, share_1, jnp.where(lane == 1, share_2, 0.0))
    tail = jnp.where(lane == 2, share_3, tail)
    even = (D // 128) * 128
    out_ref[:, :even] = piece[:, :even].astype(BF16)
    out_ref[:, even:] = jnp.concatenate([piece[:, even:], tail], axis=1).astype(BF16)


def experts_step(rows, *blocks):
    count, hid = rows.shape[0], blocks[0].shape[1] // 3
    return pl.pallas_call(
        experts_kernel,
        out_shape=jax.ShapeDtypeStruct((count // 2, PADDED), BF16),
        in_specs=[pl.BlockSpec(memory_space=pltpu.VMEM)] * (1 + len(blocks)),
        out_specs=pl.BlockSpec(memory_space=pltpu.VMEM),
        compiler_params=pltpu.CompilerParams(vmem_limit_bytes=32 << 20),
        cost_estimate=pl.CostEstimate(
            flops=len(blocks) * count * D * hid * 5,
            bytes_accessed=2 * (len(blocks) * D * 3 * hid + 2 * count * PADDED),
            transcendentals=count * hid,
        ),
    )(rows, *blocks)


def project_kernel(columns_ref, weight_ref, out_ref):
    count = columns_ref.shape[0]
    at = lax.broadcasted_iota(jnp.int32, (count // 2, count), 0)
    source = (at // SLOTS) * (2 * SLOTS) + at % SLOTS
    kept = lax.broadcasted_iota(jnp.int32, (count // 2, count), 1) == source
    rows = dot32(kept.astype(BF16), columns_ref[...]).astype(BF16)
    out_ref[...] = dot_last(rows, weight_ref[...]).astype(BF16)


def project_slots(columns, weight):
    count, lanes = columns.shape
    return pl.pallas_call(
        project_kernel,
        out_shape=jax.ShapeDtypeStruct((count // 2, D), BF16),
        in_specs=[pl.BlockSpec(memory_space=pltpu.VMEM)] * 2,
        out_specs=pl.BlockSpec(memory_space=pltpu.VMEM),
        compiler_params=pltpu.CompilerParams(vmem_limit_bytes=16 << 20),
        cost_estimate=pl.CostEstimate(
            flops=count * D * lanes,
            bytes_accessed=2 * (count * lanes + D * lanes + count * D // 2),
            transcendentals=0,
        ),
    )(columns, weight)


def shards(
    queries,
    key_rows,
    value_matrix,
    head_sink_logits,
    residual,
    out_weight,
    norm_gain,
    router,
    expert_gate,
    expert_up,
    expert_down,
    routes,
    group_ids,
    rewards,
    response_mask,
    upstream,
):
    pairs, dp_count = lax.axis_size("pair"), lax.axis_size("dp")
    seq_index = lax.axis_index(SEQ)
    query_rows = queries[0]
    tokens = query_rows.shape[0]
    group_count = max(dp_count // 4, 1)
    all_tokens = dp_count * lax.psum(1, SEQ) * tokens
    lanes = out_weight.shape[0]

    route_rows = routes[0]
    window = jnp.arange(EW, dtype=jnp.int32)
    chosen = jnp.any(route_rows[:, :, None] == window, axis=1)
    below = jnp.arange(tokens)[:, None] >= jnp.arange(tokens)[None, :]
    rank = dot32(below.astype(BF16), chosen.astype(BF16)) - 1.0
    slot_hot = chosen.T[:, None, :] & (
        rank.T[:, None, :] == jnp.arange(CAP, dtype=F32)[None, :, None]
    )
    pick = slot_hot.reshape(SLOTS, tokens)
    pick_low = pick.astype(BF16)
    slot_expert = jnp.repeat(window, CAP)

    shard = jnp.concatenate([expert_gate, expert_up, expert_down], axis=1)
    spread_shard = jnp.broadcast_to(shard[None], (dp_count, *shard.shape))
    spread_shard, own_keys, own_values, mask_row = lax.optimization_barrier(
        (spread_shard, key_rows[0], value_matrix[0], response_mask[0])
    )
    gathered = exchange(spread_shard, "dp")

    halo = along_seq(jnp.concatenate([own_keys, own_values], axis=1), 1)
    kv_width = key_rows.shape[2]
    keys_here = jnp.concatenate([halo[:, :kv_width], own_keys], axis=0)
    values_here = jnp.concatenate([halo[:, kv_width:], own_values], axis=0)
    row_index = jnp.arange(tokens, dtype=jnp.int32)[:, None]
    col_index = jnp.arange(WINDOW + tokens, dtype=jnp.int32)[None, :]

    def visible(rows, columns):
        return (
            (columns >= rows + 1)
            & (columns <= rows + WINDOW)
            & ((columns >= WINDOW) | (seq_index > 0))
        )

    slot_rows = jnp.sum(jnp.where(pick, row_index[:, 0][None, :], 0), axis=1, keepdims=True)
    query_slots = dot32(pick_low, query_rows).astype(BF16)
    probs_slots, sink_slots = head_scores(
        query_slots, keys_here, head_sink_logits, visible(slot_rows, col_index)
    )
    attended_slots = head_mix(probs_slots.astype(BF16), values_here)

    pair_count = jnp.full((8, 128), jnp.sum(mask_row.astype(F32)))
    pair_count = pair_count + swap(pair_count, "core")
    pair_count = pair_count[0, 0] + swap(pair_count, "half")[0, 0]
    pair_high = jnp.floor(pair_count / 64.0)
    facts = jnp.stack(
        [
            pair_high,
            pair_count - 64.0 * pair_high,
            rewards[0].astype(F32),
            group_ids[0].astype(F32),
        ]
    )
    facts_row = jnp.pad(facts, (0, lanes - 4))[None].astype(BF16)
    columns = attended_slots.reshape(SLOTS, dp_count, lanes).transpose(1, 0, 2)
    sent = jnp.concatenate(
        [columns, jnp.broadcast_to(facts_row[None], (dp_count, 1, lanes))], axis=1
    )
    sent = jnp.pad(sent, ((0, 0), (0, 2 * SLOTS - SLOTS - 1), (0, 0)))
    sent, gathered, late_weight = lax.optimization_barrier((sent, gathered, out_weight))
    out_full = lax.all_gather(late_weight, "dp", axis=0, tiled=True)
    arrived = exchange(sent, "dp")
    facts_all = arrived[:, SLOTS, :4].astype(F32)
    partial = project_slots(arrived.reshape(dp_count * 2 * SLOTS, lanes), out_weight.T)
    partial, residual_rows, upstream_rows, pick_low = lax.optimization_barrier(
        (partial.reshape(dp_count, SLOTS, D), residual[0], upstream[0], pick_low)
    )
    partial = exchange(partial, "dp")
    pick = pick_low > 0
    projected = jnp.sum(partial.astype(F32), axis=0)
    own_block = gathered.reshape(D, shard.shape[1])
    half_block = swap(own_block, "half")
    blocks = (own_block, half_block, swap(own_block, "core"), swap(half_block, "core"))

    residual_slots = dot32(pick_low, residual_rows)
    upstream_slots = dot32(pick_low, upstream_rows).astype(BF16)
    mid = (residual_slots + projected).astype(BF16)
    mid_wide = lax.optimization_barrier(mid).astype(F32)
    inv_rms = lax.rsqrt(jnp.mean(mid_wide * mid_wide, axis=1, keepdims=True) + NORM_EPS)
    unit_rows = mid_wide * inv_rms
    normed = (unit_rows * norm_gain[None, :]).astype(BF16)

    counts_here = jnp.sum(64.0 * facts_all[:, 0] + facts_all[:, 1])
    group_hot = (facts_all[:, 3][:, None] == jnp.arange(group_count, dtype=F32)).astype(F32)
    reward_all = facts_all[:, 2]
    group_sizes = jnp.sum(group_hot, axis=0)
    group_sums = jnp.sum(group_hot * reward_all[:, None], axis=0)
    group_squares = jnp.sum(group_hot * (reward_all * reward_all)[:, None], axis=0)
    own_hot = group_ids[0] == jnp.arange(group_count, dtype=jnp.int32)
    means = group_sums / group_sizes
    spreads = group_squares / group_sizes - means * means
    own_mean = jnp.sum(jnp.where(own_hot, means, 0.0))
    own_spread = jnp.sum(jnp.where(own_hot, spreads, 0.0))
    advantage = (rewards[0].astype(F32) - own_mean) / jnp.sqrt(jnp.maximum(own_spread, 1.0))

    count_high = jnp.floor(counts_here / 64.0)
    count_tail = jnp.stack([count_high, counts_here - 64.0 * count_high])
    count_tail = jnp.pad(count_tail, (0, PADDED - D - 2)).astype(BF16)
    tails = jnp.broadcast_to(count_tail[None], (2 * SLOTS, PADDED - D))
    both = jnp.concatenate([jnp.concatenate([normed, upstream_slots], axis=0), tails], axis=1)
    at = jnp.arange(2 * SLOTS)
    source = (at // SLOTS) * CAP + at % CAP + jnp.where(at % SLOTS >= CAP, SLOTS, 0)
    arrange = (source[:, None] == at[None, :]).astype(BF16)
    by_expert = dot32(arrange, both).astype(BF16).reshape(EW, 1, 2 * CAP, PADDED)
    query_late, normed_late, route_late, upstream_rows, pick_low, by_expert, row_late, col_late = (
        lax.optimization_barrier(
            (
                query_rows,
                normed,
                route_rows,
                upstream_rows,
                pick_low,
                by_expert,
                row_index,
                col_index,
            )
        )
    )
    pick = pick_low > 0
    same = dot_last(pick_low, pick_low)
    primary = jnp.sum(jnp.tril(same, -1), axis=1) == 0
    place = jnp.where(primary[:, None], pick, False)
    taken = jnp.any(pick, axis=0)
    outgoing = jnp.broadcast_to(by_expert, (EW, pairs // EW, 2 * CAP, PADDED))
    came = exchange(outgoing.reshape(pairs, 2 * CAP, PADDED), "pair")

    back = experts_step(came.reshape(pairs * 2 * CAP, PADDED), *blocks)
    back, mask_late = lax.optimization_barrier(
        (back.reshape(pairs, CAP, PADDED), mask_row)
    )
    mask_late = mask_late.astype(F32)
    back = exchange(back, "pair")

    masked = jnp.where(mask_late[:, None] > 0.0, upstream_rows, jnp.zeros_like(upstream_rows))
    grad_attended = jnp.where(taken[:, None], 0.0, dot_last(masked, out_full)).astype(BF16)
    came, grad_attended = lax.optimization_barrier((came, grad_attended))
    count_parts = jnp.sum(came[:, 0, D : D + 2].astype(F32), axis=0)
    token_total = count_parts[0] * 64.0 + count_parts[1]
    token_scale = -advantage * all_tokens / token_total
    loss_weight = token_scale * mask_late
    probs, sink_probs = head_scores(
        query_late, keys_here, head_sink_logits, visible(row_late, col_late)
    )
    grad_prob, spread = head_spread(probs, values_here, grad_attended)
    grad_q, grad_k, grad_v = head_grads(
        probs, grad_prob, spread, query_late, keys_here, grad_attended, token_scale
    )
    back, grad_q, grad_k, grad_v, spread = lax.optimization_barrier(
        (back, grad_q, grad_k, grad_v, spread)
    )
    dense_sinks = jnp.sum(sink_probs * spread, axis=2).reshape(QUERY_HEADS) * token_scale
    summed = jnp.sum(back.reshape(EW, pairs // EW, CAP, PADDED).astype(F32), axis=1)
    summed = summed.reshape(SLOTS, PADDED)
    share_slots = jnp.sum(summed[:, D : D + 3], axis=1)

    logits = dot32(normed_late, router)
    route_slots = dot32(pick_low, route_late.astype(BF16)).astype(jnp.int32)
    route_hot = route_slots[:, :, None] == jnp.arange(EXPERTS, dtype=jnp.int32)
    route_logits = jnp.sum(jnp.where(route_hot, logits[:, None, :], 0.0), axis=2)
    raised = jnp.exp(route_logits)
    route_weights = raised / jnp.sum(raised, axis=1, keepdims=True)
    weight_slots = jnp.sum(
        jnp.where(route_slots == slot_expert[:, None], route_weights, 0.0), axis=1
    )
    loss_slots = jnp.sum(jnp.where(pick, loss_weight[None, :], 0.0), axis=1)
    cot_slots = loss_slots[:, None] * upstream_slots.astype(F32)
    grad_rows = (weight_slots * loss_slots)[:, None] * summed[:, :D]
    grad_rows = dot32(same, grad_rows, precision=HIGHEST)
    grad_share = loss_slots * share_slots
    token_share = jnp.sum(
        same[:, :, None] * (grad_share[:, None] * (slot_expert[:, None] == window))[None], axis=1
    )
    grad_weights = jnp.sum(
        jnp.where(route_slots[:, :, None] == window, token_share[:, None, :], 0.0), axis=2
    )
    grad_route = route_weights * (
        grad_weights - jnp.sum(route_weights * grad_weights, axis=1, keepdims=True)
    )
    grad_logits = jnp.sum(jnp.where(route_hot, grad_route[:, :, None], 0.0), axis=1).astype(BF16)
    grad_normed = dot_last(grad_logits, router) + grad_rows
    grad_unit = grad_normed * norm_gain[None, :]
    grad_slots = cot_slots + inv_rms * (
        grad_unit - unit_rows * jnp.mean(grad_unit * unit_rows, axis=1, keepdims=True)
    )
    grad_slots = jnp.where(primary[:, None], grad_slots, 0.0).astype(BF16)

    attended_grad_slots = dot_last(grad_slots, out_full).astype(BF16)
    slot_prob, slot_spread = head_spread(probs_slots, values_here, attended_grad_slots)
    slot_sinks = jnp.sum(sink_slots * slot_spread, axis=2).reshape(QUERY_HEADS)
    sinks = jnp.pad(-(dense_sinks + slot_sinks), (0, 128 - QUERY_HEADS))[None]
    sinks = to_all(sinks, ("core", "dp"))
    sinks, slot_prob, upstream_rows = lax.optimization_barrier(
        (jnp.sum(sinks, axis=0), slot_prob, upstream_rows)
    )
    sinks = to_all(sinks, ("pair", "half"))
    sinks = jnp.sum(sinks, axis=0)

    slot_q, slot_k, slot_v = head_grads(
        probs_slots, slot_prob, slot_spread, query_slots, keys_here, attended_grad_slots, 1.0
    )
    grad_k = grad_k + slot_k
    grad_v = grad_v + slot_v
    onward = jnp.concatenate([grad_k[:WINDOW], grad_v[:WINDOW]], axis=1).astype(BF16)
    onward = along_seq(onward, -1).astype(F32)
    grad_key_rows = (grad_k[WINDOW:] + onward[:, :kv_width]).astype(BF16)
    grad_value_rows = (grad_v[WINDOW:] + onward[:, kv_width:]).astype(BF16)
    cot_rows = (loss_weight[:, None] * upstream_rows.astype(F32)).astype(BF16)
    put = place.astype(BF16)
    by_token = (((0,), (0,)), ((), ()))
    grad_residual = jnp.where(
        taken[:, None],
        lax.dot_general(put, grad_slots, by_token, preferred_element_type=F32).astype(BF16),
        cot_rows,
    )
    grad_q = jnp.where(
        taken[:, None],
        lax.dot_general(put, slot_q, by_token, preferred_element_type=F32).astype(BF16),
        grad_q,
    )
    return (
        grad_q[None],
        grad_key_rows[None],
        grad_value_rows[None],
        grad_residual[None],
        sinks[0, :QUERY_HEADS],
    )


def solution(mesh):
    seq, dp = mesh.shape["seq"], mesh.shape["dp"]
    split = Mesh(mesh.devices.reshape(seq // 4, 2, 2, dp), (*SEQ, "dp"))
    whole = SEQ

    return jax.shard_map(
        shards,
        mesh=split,
        in_specs=(
            P("dp", whole, None),
            P("dp", whole, None),
            P("dp", whole, None),
            P(),
            P("dp", whole, None),
            P("dp", None),
            P(),
            P(),
            P("dp", whole),
            P("dp", whole),
            P("dp", whole),
            P("dp", whole, None),
            P("dp"),
            P("dp"),
            P("dp", whole),
            P("dp", whole, None),
        ),
        out_specs=(
            P("dp", whole, None),
            P("dp", whole, None),
            P("dp", whole, None),
            P("dp", whole, None),
            P(),
        ),
        check_vma=False,
    )
```

```python
import jax
import jax.numpy as jnp
from jax import lax
from jax.experimental import pallas as pl
from jax.experimental.pallas import tpu as pltpu
from jax.sharding import Mesh, PartitionSpec as P

D = 2880
PADDED = 2944
HEAD_SIZE = 64
WINDOW = 128
EXPERTS = 128
QUERY_HEADS = 32
KEY_VALUE_HEADS = 4
EW = 2
CAP = 4
SLOTS = EW * CAP

NORM_EPS = 1e-05
GLU_SLOPE = 1.702
HIGHEST = lax.Precision.HIGHEST
SEQ = ("pair", "half", "core")
CONTRACT_LAST = (((1,), (1,)), ((), ()))
F32 = jnp.float32
BF16 = jnp.bfloat16


def dot32(a, b, **kw):
    return jnp.dot(a, b, preferred_element_type=F32, **kw)


def dot_last(a, b):
    return lax.dot_general(a, b, CONTRACT_LAST, preferred_element_type=F32)


def exchange(value, axis):
    return lax.all_to_all(value, axis, split_axis=0, concat_axis=0, tiled=True)


def to_all(value, axis):
    count = lax.psum(1, axis)
    return exchange(jnp.broadcast_to(value[None], (count, *value.shape)), axis)


def swap(value, axis):
    return lax.ppermute(value, axis, [(0, 1), (1, 0)])


def along_seq(value, steps):
    count = lax.psum(1, SEQ)
    first, last = max(0, -steps), min(count, count - steps)
    return lax.ppermute(value, SEQ, [(i, i + steps) for i in range(first, last)])


def head_scores(query_rows, key_rows, sinks, allowed):
    tokens, keys = query_rows.shape[0], key_rows.shape[0]
    per_group = QUERY_HEADS // KEY_VALUE_HEADS
    q = query_rows.reshape(tokens, KEY_VALUE_HEADS, per_group, HEAD_SIZE)
    k = key_rows.reshape(keys, KEY_VALUE_HEADS, HEAD_SIZE)
    scores = jnp.einsum("baqj,eaj->aqbe", q, k, preferred_element_type=F32) * HEAD_SIZE**-0.5
    scores = jnp.where(allowed[None, None], scores, -1e30)
    sink_column = sinks.reshape(KEY_VALUE_HEADS, per_group)[:, :, None]
    largest = jnp.maximum(jnp.max(scores, axis=3), sink_column)
    raised = jnp.where(allowed[None, None], jnp.exp(scores - largest[..., None]), 0.0)
    sink_raised = jnp.exp(sink_column - largest)
    denominator = jnp.sum(raised, axis=3) + sink_raised
    return raised / denominator[..., None], sink_raised / denominator


def head_mix(probs_low, value_rows):
    v = value_rows.reshape(value_rows.shape[0], KEY_VALUE_HEADS, HEAD_SIZE)
    mixed = jnp.einsum("amlh,hai->lami", probs_low, v, preferred_element_type=F32)
    return mixed.reshape(mixed.shape[0], QUERY_HEADS * HEAD_SIZE).astype(BF16)


def head_spread(probs, value_rows, grad_attended):
    tokens, keys = grad_attended.shape[0], value_rows.shape[0]
    per_group = QUERY_HEADS // KEY_VALUE_HEADS
    v = value_rows.reshape(keys, KEY_VALUE_HEADS, HEAD_SIZE)
    g = grad_attended.reshape(tokens, KEY_VALUE_HEADS, per_group, HEAD_SIZE)
    grad_prob = jnp.einsum("baqj,eaj->aqbe", g, v, preferred_element_type=F32)
    return grad_prob, jnp.sum(probs * grad_prob, axis=3)


def head_grads(probs, grad_prob, spread, query_rows, key_rows, grad_attended, scale):
    tokens, keys = query_rows.shape[0], key_rows.shape[0]
    per_group = QUERY_HEADS // KEY_VALUE_HEADS
    q = query_rows.reshape(tokens, KEY_VALUE_HEADS, per_group, HEAD_SIZE)
    k = key_rows.reshape(keys, KEY_VALUE_HEADS, HEAD_SIZE)
    g = grad_attended.reshape(tokens, KEY_VALUE_HEADS, per_group, HEAD_SIZE)
    grad_score = (probs * (grad_prob - spread[..., None])).astype(BF16)
    probs_low = probs.astype(BF16)
    scaling = HEAD_SIZE**-0.5 * scale
    grad_q = jnp.einsum("amlh,hai->lami", grad_score, k, preferred_element_type=F32) * scaling
    grad_k = jnp.einsum("ujko,kujm->oum", grad_score, q, preferred_element_type=F32) * scaling
    grad_v = jnp.einsum("ujko,kujm->oum", probs_low, g, preferred_element_type=F32) * scale
    return (
        grad_q.reshape(tokens, QUERY_HEADS * HEAD_SIZE).astype(BF16),
        grad_k.reshape(keys, KEY_VALUE_HEADS * HEAD_SIZE),
        grad_v.reshape(keys, KEY_VALUE_HEADS * HEAD_SIZE),
    )


def experts_kernel(rows_ref, *refs):
    blocks, out_ref = refs[:-1], refs[-1]
    count = rows_ref.shape[0]
    kept = count // 2
    hid = blocks[0].shape[1] // 3
    at = lax.broadcasted_iota(jnp.int32, (kept, count), 0)
    source = (at // CAP) * (2 * CAP) + at % CAP
    column = lax.broadcasted_iota(jnp.int32, (kept, count), 1)
    rows = rows_ref[:, :D]
    normed = dot32((column == source).astype(BF16), rows).astype(BF16)
    upstream = dot32((column == source + CAP).astype(BF16), rows).astype(BF16)
    piece = jnp.zeros((kept, D), F32)
    share = jnp.zeros((kept, 1), F32)
    for block in blocks:
        pair = block[:, : 2 * hid]
        pre = dot32(normed, pair)
        up_down = dot32(upstream, block[:, 2 * hid :])
        gate_pre, up_pre = pre[:, :hid], pre[:, hid:]
        sigmoid_gate = jax.nn.sigmoid(GLU_SLOPE * gate_pre)
        activation = ((up_pre + 1.0) * gate_pre * sigmoid_gate).astype(BF16)
        share = share + jnp.sum(activation.astype(F32) * up_down, axis=1, keepdims=True)
        grad_up = up_down * (gate_pre * sigmoid_gate)
        grad_gate = (
            up_down
            * (up_pre + 1.0)
            * (sigmoid_gate + GLU_SLOPE * gate_pre * sigmoid_gate * (1.0 - sigmoid_gate))
        )
        grads = jnp.concatenate([grad_gate, grad_up], axis=1).astype(BF16)
        piece = piece + dot_last(grads, pair)
    share_1 = share.astype(BF16).astype(F32)
    share_2 = (share - share_1).astype(BF16).astype(F32)
    share_3 = share - share_1 - share_2
    lane = lax.broadcasted_iota(jnp.int32, (kept, PADDED - D), 1)
    tail = jnp.where(lane == 0, share_1, jnp.where(lane == 1, share_2, 0.0))
    tail = jnp.where(lane == 2, share_3, tail)
    even = (D // 128) * 128
    out_ref[:, :even] = piece[:, :even].astype(BF16)
    out_ref[:, even:] = jnp.concatenate([piece[:, even:], tail], axis=1).astype(BF16)


def experts_step(rows, *blocks):
    count, hid = rows.shape[0], blocks[0].shape[1] // 3
    return pl.pallas_call(
        experts_kernel,
        out_shape=jax.ShapeDtypeStruct((count // 2, PADDED), BF16),
        in_specs=[pl.BlockSpec(memory_space=pltpu.VMEM)] * (1 + len(blocks)),
        out_specs=pl.BlockSpec(memory_space=pltpu.VMEM),
        compiler_params=pltpu.CompilerParams(vmem_limit_bytes=32 << 20),
        cost_estimate=pl.CostEstimate(
            flops=len(blocks) * count * D * hid * 5,
            bytes_accessed=2 * (len(blocks) * D * 3 * hid + 2 * count * PADDED),
            transcendentals=count * hid,
        ),
    )(rows, *blocks)


def project_kernel(columns_ref, weight_ref, out_ref):
    count = columns_ref.shape[0]
    at = lax.broadcasted_iota(jnp.int32, (count // 2, count), 0)
    source = (at // SLOTS) * (2 * SLOTS) + at % SLOTS
    kept = lax.broadcasted_iota(jnp.int32, (count // 2, count), 1) == source
    rows = dot32(kept.astype(BF16), columns_ref[...]).astype(BF16)
    out_ref[...] = dot_last(rows, weight_ref[...]).astype(BF16)


def project_slots(columns, weight):
    count, lanes = columns.shape
    return pl.pallas_call(
        project_kernel,
        out_shape=jax.ShapeDtypeStruct((count // 2, D), BF16),
        in_specs=[pl.BlockSpec(memory_space=pltpu.VMEM)] * 2,
        out_specs=pl.BlockSpec(memory_space=pltpu.VMEM),
        compiler_params=pltpu.CompilerParams(vmem_limit_bytes=16 << 20),
        cost_estimate=pl.CostEstimate(
            flops=count * D * lanes,
            bytes_accessed=2 * (count * lanes + D * lanes + count * D // 2),
            transcendentals=0,
        ),
    )(columns, weight)


def shards(
    queries,
    key_rows,
    value_matrix,
    head_sink_logits,
    residual,
    out_weight,
    norm_gain,
    router,
    expert_gate,
    expert_up,
    expert_down,
    routes,
    group_ids,
    rewards,
    response_mask,
    upstream,
):
    pairs, dp_count = lax.axis_size("pair"), lax.axis_size("dp")
    seq_index = lax.axis_index(SEQ)
    query_rows = queries[0]
    tokens = query_rows.shape[0]
    group_count = max(dp_count // 4, 1)
    all_tokens = dp_count * lax.psum(1, SEQ) * tokens
    lanes = out_weight.shape[0]

    route_rows = routes[0]
    window = jnp.arange(EW, dtype=jnp.int32)
    chosen = jnp.any(route_rows[:, :, None] == window, axis=1)
    below = jnp.arange(tokens)[:, None] >= jnp.arange(tokens)[None, :]
    rank = dot32(below.astype(BF16), chosen.astype(BF16)) - 1.0
    slot_hot = chosen.T[:, None, :] & (
        rank.T[:, None, :] == jnp.arange(CAP, dtype=F32)[None, :, None]
    )
    pick = slot_hot.reshape(SLOTS, tokens)
    pick_low = pick.astype(BF16)
    slot_expert = jnp.repeat(window, CAP)

    shard = jnp.concatenate([expert_gate, expert_up, expert_down], axis=1)
    spread_shard = jnp.broadcast_to(shard[None], (dp_count, *shard.shape))
    spread_shard, own_keys, own_values, mask_row, query_rows = lax.optimization_barrier(
        (spread_shard, key_rows[0], value_matrix[0], response_mask[0], query_rows)
    )
    gathered = exchange(spread_shard, "dp")

    halo = along_seq(jnp.concatenate([own_keys, own_values], axis=1), 1)
    kv_width = key_rows.shape[2]
    keys_here = jnp.concatenate([halo[:, :kv_width], own_keys], axis=0)
    values_here = jnp.concatenate([halo[:, kv_width:], own_values], axis=0)
    row_index = jnp.arange(tokens, dtype=jnp.int32)[:, None]
    col_index = jnp.arange(WINDOW + tokens, dtype=jnp.int32)[None, :]

    def visible(rows, columns):
        return (
            (columns >= rows + 1)
            & (columns <= rows + WINDOW)
            & ((columns >= WINDOW) | (seq_index > 0))
        )

    slot_rows = jnp.sum(jnp.where(pick, row_index[:, 0][None, :], 0), axis=1, keepdims=True)
    query_slots = dot32(pick_low, query_rows).astype(BF16)
    query_slots, late_weight = lax.optimization_barrier((query_slots, out_weight))
    out_full = lax.all_gather(late_weight, "dp", axis=0, tiled=True)
    probs_slots, sink_slots = head_scores(
        query_slots, keys_here, head_sink_logits, visible(slot_rows, col_index)
    )
    attended_slots = head_mix(probs_slots.astype(BF16), values_here)

    facts = jnp.stack(
        [
            jnp.sum(mask_row.astype(F32)),
            rewards[0].astype(F32),
            group_ids[0].astype(F32),
        ]
    )
    facts_row = jnp.pad(facts, (0, lanes - 3))[None].astype(BF16)
    columns = attended_slots.reshape(SLOTS, dp_count, lanes).transpose(1, 0, 2)
    sent = jnp.concatenate(
        [columns, jnp.broadcast_to(facts_row[None], (dp_count, 1, lanes))], axis=1
    )
    sent = jnp.pad(sent, ((0, 0), (0, 2 * SLOTS - SLOTS - 1), (0, 0)))
    sent, gathered = lax.optimization_barrier((sent, gathered))
    arrived = exchange(sent, "dp")
    facts_all = arrived[:, SLOTS, :3].astype(F32)
    partial = project_slots(arrived.reshape(dp_count * 2 * SLOTS, lanes), out_weight.T)
    partial, residual_rows, upstream_rows, pick_low = lax.optimization_barrier(
        (partial.reshape(dp_count, SLOTS, D), residual[0], upstream[0], pick_low)
    )
    partial = exchange(partial, "dp")
    pick = pick_low > 0
    projected = jnp.sum(partial.astype(F32), axis=0)
    own_block = gathered.reshape(D, shard.shape[1])
    half_block = swap(own_block, "half")
    core_block = swap(own_block, "core")
    blocks = (own_block, half_block, core_block, swap(half_block, "core"))

    residual_slots = dot32(pick_low, residual_rows)
    upstream_slots = dot32(pick_low, upstream_rows).astype(BF16)
    mid = (residual_slots + projected).astype(BF16)
    mid_wide = lax.optimization_barrier(mid).astype(F32)
    inv_rms = lax.rsqrt(jnp.mean(mid_wide * mid_wide, axis=1, keepdims=True) + NORM_EPS)
    unit_rows = mid_wide * inv_rms
    normed = (unit_rows * norm_gain[None, :]).astype(BF16)

    pair_count = jnp.full((8, 128), jnp.sum(facts_all[:, 0]))
    pair_count = pair_count + swap(pair_count, "core")
    counts_here = pair_count[0, 0] + swap(pair_count, "half")[0, 0]
    group_hot = (facts_all[:, 2][:, None] == jnp.arange(group_count, dtype=F32)).astype(F32)
    reward_all = facts_all[:, 1]
    group_sizes = jnp.sum(group_hot, axis=0)
    group_sums = jnp.sum(group_hot * reward_all[:, None], axis=0)
    group_squares = jnp.sum(group_hot * (reward_all * reward_all)[:, None], axis=0)
    own_hot = group_ids[0] == jnp.arange(group_count, dtype=jnp.int32)
    means = group_sums / group_sizes
    spreads = group_squares / group_sizes - means * means
    own_mean = jnp.sum(jnp.where(own_hot, means, 0.0))
    own_spread = jnp.sum(jnp.where(own_hot, spreads, 0.0))
    advantage = (rewards[0].astype(F32) - own_mean) / jnp.sqrt(jnp.maximum(own_spread, 1.0))

    count_high = jnp.floor(counts_here / 64.0)
    count_tail = jnp.stack([count_high, counts_here - 64.0 * count_high])
    count_tail = jnp.pad(count_tail, (0, PADDED - D - 2)).astype(BF16)
    tails = jnp.broadcast_to(count_tail[None], (2 * SLOTS, PADDED - D))
    both = jnp.concatenate([jnp.concatenate([normed, upstream_slots], axis=0), tails], axis=1)
    at = jnp.arange(2 * SLOTS)
    source = (at // SLOTS) * CAP + at % CAP + jnp.where(at % SLOTS >= CAP, SLOTS, 0)
    arrange = (source[:, None] == at[None, :]).astype(BF16)
    by_expert = dot32(arrange, both).astype(BF16).reshape(EW, 1, 2 * CAP, PADDED)
    query_late, normed_late, route_late, upstream_rows, pick_low, by_expert, row_late, col_late = (
        lax.optimization_barrier(
            (
                query_rows,
                normed,
                route_rows,
                upstream_rows,
                pick_low,
                by_expert,
                row_index,
                col_index,
            )
        )
    )
    pick = pick_low > 0
    same = dot_last(pick_low, pick_low)
    primary = jnp.sum(jnp.tril(same, -1), axis=1) == 0
    place = jnp.where(primary[:, None], pick, False)
    taken = jnp.any(pick, axis=0)
    outgoing = jnp.broadcast_to(by_expert, (EW, pairs // EW, 2 * CAP, PADDED))
    came = exchange(outgoing.reshape(pairs, 2 * CAP, PADDED), "pair")

    back = experts_step(came.reshape(pairs * 2 * CAP, PADDED), *blocks)
    back, mask_late = lax.optimization_barrier(
        (back.reshape(pairs, CAP, PADDED), mask_row)
    )
    mask_late = mask_late.astype(F32)
    back = exchange(back, "pair")

    masked = jnp.where(mask_late[:, None] > 0.0, upstream_rows, jnp.zeros_like(upstream_rows))
    grad_attended = jnp.where(taken[:, None], 0.0, dot_last(masked, out_full)).astype(BF16)
    came, grad_attended = lax.optimization_barrier((came, grad_attended))
    count_parts = jnp.sum(came[:, 0, D : D + 2].astype(F32), axis=0)
    token_total = count_parts[0] * 64.0 + count_parts[1]
    token_scale = -advantage * all_tokens / token_total
    loss_weight = token_scale * mask_late
    probs, sink_probs = head_scores(
        query_late, keys_here, head_sink_logits, visible(row_late, col_late)
    )
    grad_prob, spread = head_spread(probs, values_here, grad_attended)
    grad_q, grad_k, grad_v = head_grads(
        probs, grad_prob, spread, query_late, keys_here, grad_attended, token_scale
    )
    back, grad_q, grad_k, grad_v, spread = lax.optimization_barrier(
        (back, grad_q, grad_k, grad_v, spread)
    )
    dense_sinks = jnp.sum(sink_probs * spread, axis=2).reshape(QUERY_HEADS) * token_scale
    summed = jnp.sum(back.reshape(EW, pairs // EW, CAP, PADDED).astype(F32), axis=1)
    summed = summed.reshape(SLOTS, PADDED)
    share_slots = jnp.sum(summed[:, D : D + 3], axis=1)

    logits = dot32(normed_late, router)
    route_slots = dot32(pick_low, route_late.astype(BF16)).astype(jnp.int32)
    route_hot = route_slots[:, :, None] == jnp.arange(EXPERTS, dtype=jnp.int32)
    route_logits = jnp.sum(jnp.where(route_hot, logits[:, None, :], 0.0), axis=2)
    raised = jnp.exp(route_logits)
    route_weights = raised / jnp.sum(raised, axis=1, keepdims=True)
    weight_slots = jnp.sum(
        jnp.where(route_slots == slot_expert[:, None], route_weights, 0.0), axis=1
    )
    loss_slots = jnp.sum(jnp.where(pick, loss_weight[None, :], 0.0), axis=1)
    cot_slots = loss_slots[:, None] * upstream_slots.astype(F32)
    grad_rows = (weight_slots * loss_slots)[:, None] * summed[:, :D]
    grad_rows = dot32(same, grad_rows, precision=HIGHEST)
    grad_share = loss_slots * share_slots
    token_share = jnp.sum(
        same[:, :, None] * (grad_share[:, None] * (slot_expert[:, None] == window))[None], axis=1
    )
    grad_weights = jnp.sum(
        jnp.where(route_slots[:, :, None] == window, token_share[:, None, :], 0.0), axis=2
    )
    grad_route = route_weights * (
        grad_weights - jnp.sum(route_weights * grad_weights, axis=1, keepdims=True)
    )
    grad_logits = jnp.sum(jnp.where(route_hot, grad_route[:, :, None], 0.0), axis=1).astype(BF16)
    grad_normed = dot_last(grad_logits, router) + grad_rows
    grad_unit = grad_normed * norm_gain[None, :]
    grad_slots = cot_slots + inv_rms * (
        grad_unit - unit_rows * jnp.mean(grad_unit * unit_rows, axis=1, keepdims=True)
    )
    grad_slots = jnp.where(primary[:, None], grad_slots, 0.0).astype(BF16)

    attended_grad_slots = dot_last(grad_slots, out_full).astype(BF16)
    slot_prob, slot_spread = head_spread(probs_slots, values_here, attended_grad_slots)
    slot_sinks = jnp.sum(sink_slots * slot_spread, axis=2).reshape(QUERY_HEADS)
    sinks = jnp.pad(-(dense_sinks + slot_sinks), (0, 128 - QUERY_HEADS))[None]
    sinks = to_all(sinks, ("half", "core", "dp"))
    sinks, slot_prob, upstream_rows = lax.optimization_barrier(
        (jnp.sum(sinks, axis=0), slot_prob, upstream_rows)
    )
    sinks = to_all(sinks, "pair")
    sinks = jnp.sum(sinks, axis=0)

    slot_q, slot_k, slot_v = head_grads(
        probs_slots, slot_prob, slot_spread, query_slots, keys_here, attended_grad_slots, 1.0
    )
    grad_k = grad_k + slot_k
    grad_v = grad_v + slot_v
    onward = jnp.concatenate([grad_k[:WINDOW], grad_v[:WINDOW]], axis=1).astype(BF16)
    onward = along_seq(onward, -1).astype(F32)
    grad_key_rows = (grad_k[WINDOW:] + onward[:, :kv_width]).astype(BF16)
    grad_value_rows = (grad_v[WINDOW:] + onward[:, kv_width:]).astype(BF16)
    cot_rows = (loss_weight[:, None] * upstream_rows.astype(F32)).astype(BF16)
    put = place.astype(BF16)
    by_token = (((0,), (0,)), ((), ()))
    grad_residual = jnp.where(
        taken[:, None],
        lax.dot_general(put, grad_slots, by_token, preferred_element_type=F32).astype(BF16),
        cot_rows,
    )
    grad_q = jnp.where(
        taken[:, None],
        lax.dot_general(put, slot_q, by_token, preferred_element_type=F32).astype(BF16),
        grad_q,
    )
    return (
        grad_q[None],
        grad_key_rows[None],
        grad_value_rows[None],
        grad_residual[None],
        sinks[0, :QUERY_HEADS],
    )


def solution(mesh):
    seq, dp = mesh.shape["seq"], mesh.shape["dp"]
    split = Mesh(mesh.devices.reshape(seq // 4, 2, 2, dp), (*SEQ, "dp"))
    whole = SEQ

    return jax.shard_map(
        shards,
        mesh=split,
        in_specs=(
            P("dp", whole, None),
            P("dp", whole, None),
            P("dp", whole, None),
            P(),
            P("dp", whole, None),
            P("dp", None),
            P(),
            P(),
            P("dp", whole),
            P("dp", whole),
            P("dp", whole),
            P("dp", whole, None),
            P("dp"),
            P("dp"),
            P("dp", whole),
            P("dp", whole, None),
        ),
        out_specs=(
            P("dp", whole, None),
            P("dp", whole, None),
            P("dp", whole, None),
            P("dp", whole, None),
            P(),
        ),
        check_vma=False,
    )
```

```python
import jax
import jax.numpy as jnp
from jax import lax
from jax.experimental import pallas as pl
from jax.experimental.pallas import tpu as pltpu
from jax.sharding import Mesh, PartitionSpec as P

D = 2880
PADDED = 2944
HEAD_SIZE = 64
WINDOW = 128
EXPERTS = 128
QUERY_HEADS = 32
KEY_VALUE_HEADS = 4
EW = 2
CAP = 4
SLOTS = EW * CAP

NORM_EPS = 1e-05
GLU_SLOPE = 1.702
HIGHEST = lax.Precision.HIGHEST
SEQ = ("pair", "half", "core")
CONTRACT_LAST = (((1,), (1,)), ((), ()))
F32 = jnp.float32
BF16 = jnp.bfloat16


def dot32(a, b, **kw):
    return jnp.dot(a, b, preferred_element_type=F32, **kw)


def dot_last(a, b):
    return lax.dot_general(a, b, CONTRACT_LAST, preferred_element_type=F32)


def exchange(value, axis):
    return lax.all_to_all(value, axis, split_axis=0, concat_axis=0, tiled=True)


def to_all(value, axis):
    count = lax.psum(1, axis)
    return exchange(jnp.broadcast_to(value[None], (count, *value.shape)), axis)


def swap(value, axis):
    return lax.ppermute(value, axis, [(0, 1), (1, 0)])


def along_seq(value, steps):
    count = lax.psum(1, SEQ)
    first, last = max(0, -steps), min(count, count - steps)
    return lax.ppermute(value, SEQ, [(i, i + steps) for i in range(first, last)])


def head_scores(query_rows, key_rows, sinks, allowed):
    tokens, keys = query_rows.shape[0], key_rows.shape[0]
    per_group = QUERY_HEADS // KEY_VALUE_HEADS
    q = query_rows.reshape(tokens, KEY_VALUE_HEADS, per_group, HEAD_SIZE)
    k = key_rows.reshape(keys, KEY_VALUE_HEADS, HEAD_SIZE)
    scores = jnp.einsum("baqj,eaj->aqbe", q, k, preferred_element_type=F32) * HEAD_SIZE**-0.5
    scores = jnp.where(allowed[None, None], scores, -1e30)
    sink_column = sinks.reshape(KEY_VALUE_HEADS, per_group)[:, :, None]
    largest = jnp.maximum(jnp.max(scores, axis=3), sink_column)
    raised = jnp.where(allowed[None, None], jnp.exp(scores - largest[..., None]), 0.0)
    sink_raised = jnp.exp(sink_column - largest)
    denominator = jnp.sum(raised, axis=3) + sink_raised
    return raised / denominator[..., None], sink_raised / denominator


def head_mix(probs_low, value_rows):
    v = value_rows.reshape(value_rows.shape[0], KEY_VALUE_HEADS, HEAD_SIZE)
    mixed = jnp.einsum("amlh,hai->lami", probs_low, v, preferred_element_type=F32)
    return mixed.reshape(mixed.shape[0], QUERY_HEADS * HEAD_SIZE).astype(BF16)


def head_spread(probs, value_rows, grad_attended):
    tokens, keys = grad_attended.shape[0], value_rows.shape[0]
    per_group = QUERY_HEADS // KEY_VALUE_HEADS
    v = value_rows.reshape(keys, KEY_VALUE_HEADS, HEAD_SIZE)
    g = grad_attended.reshape(tokens, KEY_VALUE_HEADS, per_group, HEAD_SIZE)
    grad_prob = jnp.einsum("baqj,eaj->aqbe", g, v, preferred_element_type=F32)
    return grad_prob, jnp.sum(probs * grad_prob, axis=3)


def head_grads(probs, grad_prob, spread, query_rows, key_rows, grad_attended, scale):
    tokens, keys = query_rows.shape[0], key_rows.shape[0]
    per_group = QUERY_HEADS // KEY_VALUE_HEADS
    q = query_rows.reshape(tokens, KEY_VALUE_HEADS, per_group, HEAD_SIZE)
    k = key_rows.reshape(keys, KEY_VALUE_HEADS, HEAD_SIZE)
    g = grad_attended.reshape(tokens, KEY_VALUE_HEADS, per_group, HEAD_SIZE)
    grad_score = (probs * (grad_prob - spread[..., None])).astype(BF16)
    probs_low = probs.astype(BF16)
    scaling = HEAD_SIZE**-0.5 * scale
    grad_q = jnp.einsum("amlh,hai->lami", grad_score, k, preferred_element_type=F32) * scaling
    grad_k = jnp.einsum("ujko,kujm->oum", grad_score, q, preferred_element_type=F32) * scaling
    grad_v = jnp.einsum("ujko,kujm->oum", probs_low, g, preferred_element_type=F32) * scale
    return (
        grad_q.reshape(tokens, QUERY_HEADS * HEAD_SIZE).astype(BF16),
        grad_k.reshape(keys, KEY_VALUE_HEADS * HEAD_SIZE),
        grad_v.reshape(keys, KEY_VALUE_HEADS * HEAD_SIZE),
    )


def experts_kernel(rows_ref, *refs):
    blocks, out_ref = refs[:-1], refs[-1]
    count = rows_ref.shape[0]
    kept = count // 2
    hid = blocks[0].shape[1] // 3
    at = lax.broadcasted_iota(jnp.int32, (kept, count), 0)
    source = (at // CAP) * (2 * CAP) + at % CAP
    column = lax.broadcasted_iota(jnp.int32, (kept, count), 1)
    rows = rows_ref[:, :D]
    normed = dot32((column == source).astype(BF16), rows).astype(BF16)
    upstream = dot32((column == source + CAP).astype(BF16), rows).astype(BF16)
    piece = jnp.zeros((kept, D), F32)
    share = jnp.zeros((kept, 1), F32)
    for block in blocks:
        pair = block[:, : 2 * hid]
        pre = dot32(normed, pair)
        up_down = dot32(upstream, block[:, 2 * hid :])
        gate_pre, up_pre = pre[:, :hid], pre[:, hid:]
        sigmoid_gate = jax.nn.sigmoid(GLU_SLOPE * gate_pre)
        activation = ((up_pre + 1.0) * gate_pre * sigmoid_gate).astype(BF16)
        share = share + jnp.sum(activation.astype(F32) * up_down, axis=1, keepdims=True)
        grad_up = up_down * (gate_pre * sigmoid_gate)
        grad_gate = (
            up_down
            * (up_pre + 1.0)
            * (sigmoid_gate + GLU_SLOPE * gate_pre * sigmoid_gate * (1.0 - sigmoid_gate))
        )
        grads = jnp.concatenate([grad_gate, grad_up], axis=1).astype(BF16)
        piece = piece + dot_last(grads, pair)
    share_1 = share.astype(BF16).astype(F32)
    share_2 = (share - share_1).astype(BF16).astype(F32)
    share_3 = share - share_1 - share_2
    lane = lax.broadcasted_iota(jnp.int32, (kept, PADDED - D), 1)
    tail = jnp.where(lane == 0, share_1, jnp.where(lane == 1, share_2, 0.0))
    tail = jnp.where(lane == 2, share_3, tail)
    even = (D // 128) * 128
    out_ref[:, :even] = piece[:, :even].astype(BF16)
    out_ref[:, even:] = jnp.concatenate([piece[:, even:], tail], axis=1).astype(BF16)


def experts_step(rows, *blocks):
    count, hid = rows.shape[0], blocks[0].shape[1] // 3
    return pl.pallas_call(
        experts_kernel,
        out_shape=jax.ShapeDtypeStruct((count // 2, PADDED), BF16),
        in_specs=[pl.BlockSpec(memory_space=pltpu.VMEM)] * (1 + len(blocks)),
        out_specs=pl.BlockSpec(memory_space=pltpu.VMEM),
        compiler_params=pltpu.CompilerParams(vmem_limit_bytes=32 << 20),
        cost_estimate=pl.CostEstimate(
            flops=len(blocks) * count * D * hid * 5,
            bytes_accessed=2 * (len(blocks) * D * 3 * hid + 2 * count * PADDED),
            transcendentals=count * hid,
        ),
    )(rows, *blocks)


def project_kernel(columns_ref, weight_ref, out_ref):
    count = columns_ref.shape[0]
    at = lax.broadcasted_iota(jnp.int32, (count // 2, count), 0)
    source = (at // SLOTS) * (2 * SLOTS) + at % SLOTS
    kept = lax.broadcasted_iota(jnp.int32, (count // 2, count), 1) == source
    rows = dot32(kept.astype(BF16), columns_ref[...]).astype(BF16)
    out_ref[...] = dot_last(rows, weight_ref[...]).astype(BF16)


def project_slots(columns, weight):
    count, lanes = columns.shape
    return pl.pallas_call(
        project_kernel,
        out_shape=jax.ShapeDtypeStruct((count // 2, D), BF16),
        in_specs=[pl.BlockSpec(memory_space=pltpu.VMEM)] * 2,
        out_specs=pl.BlockSpec(memory_space=pltpu.VMEM),
        compiler_params=pltpu.CompilerParams(vmem_limit_bytes=16 << 20),
        cost_estimate=pl.CostEstimate(
            flops=count * D * lanes,
            bytes_accessed=2 * (count * lanes + D * lanes + count * D // 2),
            transcendentals=0,
        ),
    )(columns, weight)


def shards(
    queries,
    key_rows,
    value_matrix,
    head_sink_logits,
    residual,
    out_weight,
    norm_gain,
    router,
    expert_gate,
    expert_up,
    expert_down,
    routes,
    group_ids,
    rewards,
    response_mask,
    upstream,
):
    pairs, dp_count = lax.axis_size("pair"), lax.axis_size("dp")
    seq_index = lax.axis_index(SEQ)
    query_rows = queries[0]
    tokens = query_rows.shape[0]
    group_count = max(dp_count // 4, 1)
    all_tokens = dp_count * lax.psum(1, SEQ) * tokens
    lanes = out_weight.shape[0]

    route_rows = routes[0]
    window = jnp.arange(EW, dtype=jnp.int32)
    chosen = jnp.any(route_rows[:, :, None] == window, axis=1)
    below = jnp.arange(tokens)[:, None] >= jnp.arange(tokens)[None, :]
    rank = dot32(below.astype(BF16), chosen.astype(BF16)) - 1.0
    slot_hot = chosen.T[:, None, :] & (
        rank.T[:, None, :] == jnp.arange(CAP, dtype=F32)[None, :, None]
    )
    pick = slot_hot.reshape(SLOTS, tokens)
    pick_low = pick.astype(BF16)
    slot_expert = jnp.repeat(window, CAP)

    shard = jnp.concatenate([expert_gate, expert_up, expert_down], axis=1)
    spread_shard = jnp.broadcast_to(shard[None], (dp_count, *shard.shape))
    spread_shard, own_keys, own_values, mask_row, query_rows = lax.optimization_barrier(
        (spread_shard, key_rows[0], value_matrix[0], response_mask[0], query_rows)
    )
    gathered = exchange(spread_shard, "dp")

    halo = along_seq(jnp.concatenate([own_keys, own_values], axis=1), 1)
    kv_width = key_rows.shape[2]
    keys_here = jnp.concatenate([halo[:, :kv_width], own_keys], axis=0)
    values_here = jnp.concatenate([halo[:, kv_width:], own_values], axis=0)
    row_index = jnp.arange(tokens, dtype=jnp.int32)[:, None]
    col_index = jnp.arange(WINDOW + tokens, dtype=jnp.int32)[None, :]

    def visible(rows, columns):
        return (
            (columns >= rows + 1)
            & (columns <= rows + WINDOW)
            & ((columns >= WINDOW) | (seq_index > 0))
        )

    slot_rows = jnp.sum(jnp.where(pick, row_index[:, 0][None, :], 0), axis=1, keepdims=True)
    query_slots = dot32(pick_low, query_rows).astype(BF16)
    query_slots, late_weight = lax.optimization_barrier((query_slots, out_weight))
    out_full = lax.all_gather(late_weight, "dp", axis=0, tiled=True)
    probs_slots, sink_slots = head_scores(
        query_slots, keys_here, head_sink_logits, visible(slot_rows, col_index)
    )
    attended_slots = head_mix(probs_slots.astype(BF16), values_here)

    pair_count = jnp.full((8, 128), jnp.sum(mask_row.astype(F32)))
    pair_count = pair_count + swap(pair_count, "core")
    pair_count = pair_count[0, 0] + swap(pair_count, "half")[0, 0]
    pair_high = jnp.floor(pair_count / 64.0)
    facts = jnp.stack(
        [
            pair_high,
            pair_count - 64.0 * pair_high,
            rewards[0].astype(F32),
            group_ids[0].astype(F32),
        ]
    )
    facts_row = jnp.pad(facts, (0, lanes - 4))[None].astype(BF16)
    columns = attended_slots.reshape(SLOTS, dp_count, lanes).transpose(1, 0, 2)
    sent = jnp.concatenate(
        [columns, jnp.broadcast_to(facts_row[None], (dp_count, 1, lanes))], axis=1
    )
    sent = jnp.pad(sent, ((0, 0), (0, 2 * SLOTS - SLOTS - 1), (0, 0)))
    sent, gathered = lax.optimization_barrier((sent, gathered))
    arrived = exchange(sent, "dp")
    facts_all = arrived[:, SLOTS, :4].astype(F32)
    partial = project_slots(arrived.reshape(dp_count * 2 * SLOTS, lanes), out_weight.T)
    partial, residual_rows, upstream_rows, pick_low = lax.optimization_barrier(
        (partial.reshape(dp_count, SLOTS, D), residual[0], upstream[0], pick_low)
    )
    partial = exchange(partial, "dp")
    pick = pick_low > 0
    projected = jnp.sum(partial.astype(F32), axis=0)
    own_block = gathered.reshape(D, shard.shape[1])
    half_block = swap(own_block, "half")
    core_block = swap(own_block, "core")
    blocks = (own_block, half_block, core_block, swap(half_block, "core"))

    residual_slots = dot32(pick_low, residual_rows)
    upstream_slots = dot32(pick_low, upstream_rows).astype(BF16)
    mid = (residual_slots + projected).astype(BF16)
    mid_wide = lax.optimization_barrier(mid).astype(F32)
    inv_rms = lax.rsqrt(jnp.mean(mid_wide * mid_wide, axis=1, keepdims=True) + NORM_EPS)
    unit_rows = mid_wide * inv_rms
    normed = (unit_rows * norm_gain[None, :]).astype(BF16)

    counts_here = jnp.sum(64.0 * facts_all[:, 0] + facts_all[:, 1])
    group_hot = (facts_all[:, 3][:, None] == jnp.arange(group_count, dtype=F32)).astype(F32)
    reward_all = facts_all[:, 2]
    group_sizes = jnp.sum(group_hot, axis=0)
    group_sums = jnp.sum(group_hot * reward_all[:, None], axis=0)
    group_squares = jnp.sum(group_hot * (reward_all * reward_all)[:, None], axis=0)
    own_hot = group_ids[0] == jnp.arange(group_count, dtype=jnp.int32)
    means = group_sums / group_sizes
    spreads = group_squares / group_sizes - means * means
    own_mean = jnp.sum(jnp.where(own_hot, means, 0.0))
    own_spread = jnp.sum(jnp.where(own_hot, spreads, 0.0))
    advantage = (rewards[0].astype(F32) - own_mean) / jnp.sqrt(jnp.maximum(own_spread, 1.0))

    count_high = jnp.floor(counts_here / 64.0)
    count_tail = jnp.stack([count_high, counts_here - 64.0 * count_high])
    count_tail = jnp.pad(count_tail, (0, PADDED - D - 2)).astype(BF16)
    tails = jnp.broadcast_to(count_tail[None], (2 * SLOTS, PADDED - D))
    both = jnp.concatenate([jnp.concatenate([normed, upstream_slots], axis=0), tails], axis=1)
    at = jnp.arange(2 * SLOTS)
    source = (at // SLOTS) * CAP + at % CAP + jnp.where(at % SLOTS >= CAP, SLOTS, 0)
    arrange = (source[:, None] == at[None, :]).astype(BF16)
    by_expert = dot32(arrange, both).astype(BF16).reshape(EW, 1, 2 * CAP, PADDED)
    query_late, normed_late, route_late, upstream_rows, pick_low, by_expert, row_late, col_late = (
        lax.optimization_barrier(
            (
                query_rows,
                normed,
                route_rows,
                upstream_rows,
                pick_low,
                by_expert,
                row_index,
                col_index,
            )
        )
    )
    pick = pick_low > 0
    same = dot_last(pick_low, pick_low)
    primary = jnp.sum(jnp.tril(same, -1), axis=1) == 0
    place = jnp.where(primary[:, None], pick, False)
    taken = jnp.any(pick, axis=0)
    outgoing = jnp.broadcast_to(by_expert, (EW, pairs // EW, 2 * CAP, PADDED))
    came = exchange(outgoing.reshape(pairs, 2 * CAP, PADDED), "pair")

    back = experts_step(came.reshape(pairs * 2 * CAP, PADDED), *blocks)
    back, mask_late = lax.optimization_barrier(
        (back.reshape(pairs, CAP, PADDED), mask_row)
    )
    mask_late = mask_late.astype(F32)
    back = exchange(back, "pair")

    masked = jnp.where(mask_late[:, None] > 0.0, upstream_rows, jnp.zeros_like(upstream_rows))
    grad_attended = jnp.where(taken[:, None], 0.0, dot_last(masked, out_full)).astype(BF16)
    came, grad_attended = lax.optimization_barrier((came, grad_attended))
    count_parts = jnp.sum(came[:, 0, D : D + 2].astype(F32), axis=0)
    token_total = count_parts[0] * 64.0 + count_parts[1]
    token_scale = -advantage * all_tokens / token_total
    loss_weight = token_scale * mask_late
    probs, sink_probs = head_scores(
        query_late, keys_here, head_sink_logits, visible(row_late, col_late)
    )
    grad_prob, spread = head_spread(probs, values_here, grad_attended)
    grad_q, grad_k, grad_v = head_grads(
        probs, grad_prob, spread, query_late, keys_here, grad_attended, token_scale
    )
    back, grad_q, grad_k, grad_v, spread = lax.optimization_barrier(
        (back, grad_q, grad_k, grad_v, spread)
    )
    dense_sinks = jnp.sum(sink_probs * spread, axis=2).reshape(QUERY_HEADS) * token_scale
    summed = jnp.sum(back.reshape(EW, pairs // EW, CAP, PADDED).astype(F32), axis=1)
    summed = summed.reshape(SLOTS, PADDED)
    share_slots = jnp.sum(summed[:, D : D + 3], axis=1)

    logits = dot32(normed_late, router)
    route_slots = dot32(pick_low, route_late.astype(BF16)).astype(jnp.int32)
    route_hot = route_slots[:, :, None] == jnp.arange(EXPERTS, dtype=jnp.int32)
    route_logits = jnp.sum(jnp.where(route_hot, logits[:, None, :], 0.0), axis=2)
    raised = jnp.exp(route_logits)
    route_weights = raised / jnp.sum(raised, axis=1, keepdims=True)
    weight_slots = jnp.sum(
        jnp.where(route_slots == slot_expert[:, None], route_weights, 0.0), axis=1
    )
    loss_slots = jnp.sum(jnp.where(pick, loss_weight[None, :], 0.0), axis=1)
    cot_slots = loss_slots[:, None] * upstream_slots.astype(F32)
    grad_rows = (weight_slots * loss_slots)[:, None] * summed[:, :D]
    grad_rows = dot32(same, grad_rows, precision=HIGHEST)
    grad_share = loss_slots * share_slots
    token_share = jnp.sum(
        same[:, :, None] * (grad_share[:, None] * (slot_expert[:, None] == window))[None], axis=1
    )
    grad_weights = jnp.sum(
        jnp.where(route_slots[:, :, None] == window, token_share[:, None, :], 0.0), axis=2
    )
    grad_route = route_weights * (
        grad_weights - jnp.sum(route_weights * grad_weights, axis=1, keepdims=True)
    )
    grad_logits = jnp.sum(jnp.where(route_hot, grad_route[:, :, None], 0.0), axis=1).astype(BF16)
    grad_normed = dot_last(grad_logits, router) + grad_rows
    grad_unit = grad_normed * norm_gain[None, :]
    grad_slots = cot_slots + inv_rms * (
        grad_unit - unit_rows * jnp.mean(grad_unit * unit_rows, axis=1, keepdims=True)
    )
    grad_slots = jnp.where(primary[:, None], grad_slots, 0.0).astype(BF16)

    attended_grad_slots = dot_last(grad_slots, out_full).astype(BF16)
    slot_prob, slot_spread = head_spread(probs_slots, values_here, attended_grad_slots)
    slot_sinks = jnp.sum(sink_slots * slot_spread, axis=2).reshape(QUERY_HEADS)
    sinks = jnp.pad(-(dense_sinks + slot_sinks), (0, 128 - QUERY_HEADS))[None]
    sinks = to_all(sinks, ("core", "dp"))
    sinks, slot_prob, upstream_rows = lax.optimization_barrier(
        (jnp.sum(sinks, axis=0), slot_prob, upstream_rows)
    )
    sinks = to_all(sinks, ("pair", "half"))
    sinks = jnp.sum(sinks, axis=0)

    slot_q, slot_k, slot_v = head_grads(
        probs_slots, slot_prob, slot_spread, query_slots, keys_here, attended_grad_slots, 1.0
    )
    grad_k = grad_k + slot_k
    grad_v = grad_v + slot_v
    onward = jnp.concatenate([grad_k[:WINDOW], grad_v[:WINDOW]], axis=1).astype(BF16)
    onward = along_seq(onward, -1).astype(F32)
    grad_key_rows = (grad_k[WINDOW:] + onward[:, :kv_width]).astype(BF16)
    grad_value_rows = (grad_v[WINDOW:] + onward[:, kv_width:]).astype(BF16)
    cot_rows = (loss_weight[:, None] * upstream_rows.astype(F32)).astype(BF16)
    put = place.astype(BF16)
    by_token = (((0,), (0,)), ((), ()))
    grad_residual = jnp.where(
        taken[:, None],
        lax.dot_general(put, grad_slots, by_token, preferred_element_type=F32).astype(BF16),
        cot_rows,
    )
    grad_q = jnp.where(
        taken[:, None],
        lax.dot_general(put, slot_q, by_token, preferred_element_type=F32).astype(BF16),
        grad_q,
    )
    return (
        grad_q[None],
        grad_key_rows[None],
        grad_value_rows[None],
        grad_residual[None],
        sinks[0, :QUERY_HEADS],
    )


def solution(mesh):
    seq, dp = mesh.shape["seq"], mesh.shape["dp"]
    split = Mesh(mesh.devices.reshape(seq // 4, 2, 2, dp), (*SEQ, "dp"))
    whole = SEQ

    return jax.shard_map(
        shards,
        mesh=split,
        in_specs=(
            P("dp", whole, None),
            P("dp", whole, None),
            P("dp", whole, None),
            P(),
            P("dp", whole, None),
            P("dp", None),
            P(),
            P(),
            P("dp", whole),
            P("dp", whole),
            P("dp", whole),
            P("dp", whole, None),
            P("dp"),
            P("dp"),
            P("dp", whole),
            P("dp", whole, None),
        ),
        out_specs=(
            P("dp", whole, None),
            P("dp", whole, None),
            P("dp", whole, None),
            P("dp", whole, None),
            P(),
        ),
        check_vma=False,
    )
```

```python
import jax
import jax.numpy as jnp
from jax import lax
from jax.experimental import pallas as pl
from jax.experimental.pallas import tpu as pltpu
from jax.sharding import Mesh, PartitionSpec as P

D = 2880
PADDED = 2944
HEAD_SIZE = 64
WINDOW = 128
EXPERTS = 128
QUERY_HEADS = 32
KEY_VALUE_HEADS = 4
EW = 2
CAP = 4
SLOTS = EW * CAP

NORM_EPS = 1e-05
GLU_SLOPE = 1.702
HIGHEST = lax.Precision.HIGHEST
SEQ = ("pair", "half", "core")
CONTRACT_LAST = (((1,), (1,)), ((), ()))
F32 = jnp.float32
BF16 = jnp.bfloat16


def dot32(a, b, **kw):
    return jnp.dot(a, b, preferred_element_type=F32, **kw)


def dot_last(a, b):
    return lax.dot_general(a, b, CONTRACT_LAST, preferred_element_type=F32)


def exchange(value, axis):
    return lax.all_to_all(value, axis, split_axis=0, concat_axis=0, tiled=True)


def to_all(value, axis):
    count = lax.psum(1, axis)
    return exchange(jnp.broadcast_to(value[None], (count, *value.shape)), axis)


def swap(value, axis):
    return lax.ppermute(value, axis, [(0, 1), (1, 0)])


def along_seq(value, steps):
    count = lax.psum(1, SEQ)
    first, last = max(0, -steps), min(count, count - steps)
    return lax.ppermute(value, SEQ, [(i, i + steps) for i in range(first, last)])


def head_scores(query_rows, key_rows, sinks, allowed):
    tokens, keys = query_rows.shape[0], key_rows.shape[0]
    per_group = QUERY_HEADS // KEY_VALUE_HEADS
    q = query_rows.reshape(tokens, KEY_VALUE_HEADS, per_group, HEAD_SIZE)
    k = key_rows.reshape(keys, KEY_VALUE_HEADS, HEAD_SIZE)
    scores = jnp.einsum("baqj,eaj->aqbe", q, k, preferred_element_type=F32) * HEAD_SIZE**-0.5
    scores = jnp.where(allowed[None, None], scores, -1e30)
    sink_column = sinks.reshape(KEY_VALUE_HEADS, per_group)[:, :, None]
    largest = jnp.maximum(jnp.max(scores, axis=3), sink_column)
    raised = jnp.where(allowed[None, None], jnp.exp(scores - largest[..., None]), 0.0)
    sink_raised = jnp.exp(sink_column - largest)
    denominator = jnp.sum(raised, axis=3) + sink_raised
    return raised / denominator[..., None], sink_raised / denominator


def head_mix(probs_low, value_rows):
    v = value_rows.reshape(value_rows.shape[0], KEY_VALUE_HEADS, HEAD_SIZE)
    mixed = jnp.einsum("amlh,hai->lami", probs_low, v, preferred_element_type=F32)
    return mixed.reshape(mixed.shape[0], QUERY_HEADS * HEAD_SIZE).astype(BF16)


def head_spread(probs, value_rows, grad_attended):
    tokens, keys = grad_attended.shape[0], value_rows.shape[0]
    per_group = QUERY_HEADS // KEY_VALUE_HEADS
    v = value_rows.reshape(keys, KEY_VALUE_HEADS, HEAD_SIZE)
    g = grad_attended.reshape(tokens, KEY_VALUE_HEADS, per_group, HEAD_SIZE)
    grad_prob = jnp.einsum("baqj,eaj->aqbe", g, v, preferred_element_type=F32)
    return grad_prob, jnp.sum(probs * grad_prob, axis=3)


def head_grads(probs, grad_prob, spread, query_rows, key_rows, grad_attended, scale):
    tokens, keys = query_rows.shape[0], key_rows.shape[0]
    per_group = QUERY_HEADS // KEY_VALUE_HEADS
    q = query_rows.reshape(tokens, KEY_VALUE_HEADS, per_group, HEAD_SIZE)
    k = key_rows.reshape(keys, KEY_VALUE_HEADS, HEAD_SIZE)
    g = grad_attended.reshape(tokens, KEY_VALUE_HEADS, per_group, HEAD_SIZE)
    grad_score = (probs * (grad_prob - spread[..., None])).astype(BF16)
    probs_low = probs.astype(BF16)
    scaling = HEAD_SIZE**-0.5 * scale
    grad_q = jnp.einsum("amlh,hai->lami", grad_score, k, preferred_element_type=F32) * scaling
    grad_k = jnp.einsum("ujko,kujm->oum", grad_score, q, preferred_element_type=F32) * scaling
    grad_v = jnp.einsum("ujko,kujm->oum", probs_low, g, preferred_element_type=F32) * scale
    return (
        grad_q.reshape(tokens, QUERY_HEADS * HEAD_SIZE).astype(BF16),
        grad_k.reshape(keys, KEY_VALUE_HEADS * HEAD_SIZE),
        grad_v.reshape(keys, KEY_VALUE_HEADS * HEAD_SIZE),
    )


def experts_kernel(rows_ref, *refs):
    blocks, out_ref = refs[:-1], refs[-1]
    count = rows_ref.shape[0]
    kept = count // 2
    hid = blocks[0].shape[1] // 3
    at = lax.broadcasted_iota(jnp.int32, (kept, count), 0)
    source = (at // CAP) * (2 * CAP) + at % CAP
    column = lax.broadcasted_iota(jnp.int32, (kept, count), 1)
    rows = rows_ref[:, :D]
    normed = dot32((column == source).astype(BF16), rows).astype(BF16)
    upstream = dot32((column == source + CAP).astype(BF16), rows).astype(BF16)
    piece = jnp.zeros((kept, D), F32)
    share = jnp.zeros((kept, 1), F32)
    for block in blocks:
        pair = block[:, : 2 * hid]
        pre = dot32(normed, pair)
        up_down = dot32(upstream, block[:, 2 * hid :])
        gate_pre, up_pre = pre[:, :hid], pre[:, hid:]
        sigmoid_gate = jax.nn.sigmoid(GLU_SLOPE * gate_pre)
        activation = ((up_pre + 1.0) * gate_pre * sigmoid_gate).astype(BF16)
        share = share + jnp.sum(activation.astype(F32) * up_down, axis=1, keepdims=True)
        grad_up = up_down * (gate_pre * sigmoid_gate)
        grad_gate = (
            up_down
            * (up_pre + 1.0)
            * (sigmoid_gate + GLU_SLOPE * gate_pre * sigmoid_gate * (1.0 - sigmoid_gate))
        )
        grads = jnp.concatenate([grad_gate, grad_up], axis=1).astype(BF16)
        piece = piece + dot_last(grads, pair)
    share_1 = share.astype(BF16).astype(F32)
    share_2 = (share - share_1).astype(BF16).astype(F32)
    share_3 = share - share_1 - share_2
    lane = lax.broadcasted_iota(jnp.int32, (kept, PADDED - D), 1)
    tail = jnp.where(lane == 0, share_1, jnp.where(lane == 1, share_2, 0.0))
    tail = jnp.where(lane == 2, share_3, tail)
    even = (D // 128) * 128
    out_ref[:, :even] = piece[:, :even].astype(BF16)
    out_ref[:, even:] = jnp.concatenate([piece[:, even:], tail], axis=1).astype(BF16)


def experts_step(rows, *blocks):
    count, hid = rows.shape[0], blocks[0].shape[1] // 3
    return pl.pallas_call(
        experts_kernel,
        out_shape=jax.ShapeDtypeStruct((count // 2, PADDED), BF16),
        in_specs=[pl.BlockSpec(memory_space=pltpu.VMEM)] * (1 + len(blocks)),
        out_specs=pl.BlockSpec(memory_space=pltpu.VMEM),
        compiler_params=pltpu.CompilerParams(vmem_limit_bytes=32 << 20),
        cost_estimate=pl.CostEstimate(
            flops=len(blocks) * count * D * hid * 5,
            bytes_accessed=2 * (len(blocks) * D * 3 * hid + 2 * count * PADDED),
            transcendentals=count * hid,
        ),
    )(rows, *blocks)


def project_kernel(columns_ref, weight_ref, out_ref):
    count = columns_ref.shape[0]
    at = lax.broadcasted_iota(jnp.int32, (count // 2, count), 0)
    source = (at // SLOTS) * (2 * SLOTS) + at % SLOTS
    kept = lax.broadcasted_iota(jnp.int32, (count // 2, count), 1) == source
    rows = dot32(kept.astype(BF16), columns_ref[...]).astype(BF16)
    out_ref[...] = dot_last(rows, weight_ref[...]).astype(BF16)


def project_slots(columns, weight):
    count, lanes = columns.shape
    return pl.pallas_call(
        project_kernel,
        out_shape=jax.ShapeDtypeStruct((count // 2, D), BF16),
        in_specs=[pl.BlockSpec(memory_space=pltpu.VMEM)] * 2,
        out_specs=pl.BlockSpec(memory_space=pltpu.VMEM),
        compiler_params=pltpu.CompilerParams(vmem_limit_bytes=16 << 20),
        cost_estimate=pl.CostEstimate(
            flops=count * D * lanes,
            bytes_accessed=2 * (count * lanes + D * lanes + count * D // 2),
            transcendentals=0,
        ),
    )(columns, weight)


def shards(
    queries,
    key_rows,
    value_matrix,
    head_sink_logits,
    residual,
    out_weight,
    norm_gain,
    router,
    expert_gate,
    expert_up,
    expert_down,
    routes,
    group_ids,
    rewards,
    response_mask,
    upstream,
):
    pairs, dp_count = lax.axis_size("pair"), lax.axis_size("dp")
    seq_index = lax.axis_index(SEQ)
    query_rows = queries[0]
    tokens = query_rows.shape[0]
    group_count = max(dp_count // 4, 1)
    all_tokens = dp_count * lax.psum(1, SEQ) * tokens
    lanes = out_weight.shape[0]

    route_rows = routes[0]
    window = jnp.arange(EW, dtype=jnp.int32)
    chosen = jnp.any(route_rows[:, :, None] == window, axis=1)
    below = jnp.arange(tokens)[:, None] >= jnp.arange(tokens)[None, :]
    rank = dot32(below.astype(BF16), chosen.astype(BF16)) - 1.0
    slot_hot = chosen.T[:, None, :] & (
        rank.T[:, None, :] == jnp.arange(CAP, dtype=F32)[None, :, None]
    )
    pick = slot_hot.reshape(SLOTS, tokens)
    pick_low = pick.astype(BF16)
    slot_expert = jnp.repeat(window, CAP)

    shard = jnp.concatenate([expert_gate, expert_up, expert_down], axis=1)
    spread_shard = jnp.broadcast_to(shard[None], (dp_count, *shard.shape))
    spread_shard, own_keys, own_values, mask_row, query_rows = lax.optimization_barrier(
        (spread_shard, key_rows[0], value_matrix[0], response_mask[0], query_rows)
    )
    gathered = exchange(spread_shard, "dp")

    halo = along_seq(jnp.concatenate([own_keys, own_values], axis=1), 1)
    kv_width = key_rows.shape[2]
    keys_here = jnp.concatenate([halo[:, :kv_width], own_keys], axis=0)
    values_here = jnp.concatenate([halo[:, kv_width:], own_values], axis=0)
    row_index = jnp.arange(tokens, dtype=jnp.int32)[:, None]
    col_index = jnp.arange(WINDOW + tokens, dtype=jnp.int32)[None, :]

    def visible(rows, columns):
        return (
            (columns >= rows + 1)
            & (columns <= rows + WINDOW)
            & ((columns >= WINDOW) | (seq_index > 0))
        )

    slot_rows = jnp.sum(jnp.where(pick, row_index[:, 0][None, :], 0), axis=1, keepdims=True)
    query_slots = dot32(pick_low, query_rows).astype(BF16)
    query_slots, late_weight = lax.optimization_barrier((query_slots, out_weight))
    out_full = lax.all_gather(late_weight, "dp", axis=0, tiled=True)
    probs_slots, sink_slots = head_scores(
        query_slots, keys_here, head_sink_logits, visible(slot_rows, col_index)
    )
    attended_slots = head_mix(probs_slots.astype(BF16), values_here)

    pair_count = jnp.full((8, 128), jnp.sum(mask_row.astype(F32)))
    pair_count = pair_count + swap(pair_count, "core")
    pair_count = pair_count[0, 0] + swap(pair_count, "half")[0, 0]
    pair_high = jnp.floor(pair_count / 64.0)
    facts = jnp.stack(
        [
            pair_high,
            pair_count - 64.0 * pair_high,
            rewards[0].astype(F32),
            group_ids[0].astype(F32),
        ]
    )
    facts_row = jnp.pad(facts, (0, lanes - 4))[None].astype(BF16)
    columns = attended_slots.reshape(SLOTS, dp_count, lanes).transpose(1, 0, 2)
    sent = jnp.concatenate(
        [columns, jnp.broadcast_to(facts_row[None], (dp_count, 1, lanes))], axis=1
    )
    sent = jnp.pad(sent, ((0, 0), (0, 2 * SLOTS - SLOTS - 1), (0, 0)))
    sent, gathered = lax.optimization_barrier((sent, gathered))
    arrived = exchange(sent, "dp")
    facts_all = arrived[:, SLOTS, :4].astype(F32)
    partial = project_slots(arrived.reshape(dp_count * 2 * SLOTS, lanes), out_weight.T)
    partial, residual_rows, upstream_rows, pick_low = lax.optimization_barrier(
        (partial.reshape(dp_count, SLOTS, D), residual[0], upstream[0], pick_low)
    )
    partial = exchange(partial, "dp")
    pick = pick_low > 0
    projected = jnp.sum(partial.astype(F32), axis=0)
    own_block = gathered.reshape(D, shard.shape[1])
    half_block = swap(own_block, "half")
    core_block = swap(own_block, "core")
    blocks = (own_block, half_block, core_block, swap(half_block, "core"))

    residual_slots = dot32(pick_low, residual_rows)
    upstream_slots = dot32(pick_low, upstream_rows).astype(BF16)
    mid = (residual_slots + projected).astype(BF16)
    mid_wide = lax.optimization_barrier(mid).astype(F32)
    inv_rms = lax.rsqrt(jnp.mean(mid_wide * mid_wide, axis=1, keepdims=True) + NORM_EPS)
    unit_rows = mid_wide * inv_rms
    normed = (unit_rows * norm_gain[None, :]).astype(BF16)

    counts_here = jnp.sum(64.0 * facts_all[:, 0] + facts_all[:, 1])
    group_hot = (facts_all[:, 3][:, None] == jnp.arange(group_count, dtype=F32)).astype(F32)
    reward_all = facts_all[:, 2]
    group_sizes = jnp.sum(group_hot, axis=0)
    group_sums = jnp.sum(group_hot * reward_all[:, None], axis=0)
    group_squares = jnp.sum(group_hot * (reward_all * reward_all)[:, None], axis=0)
    own_hot = group_ids[0] == jnp.arange(group_count, dtype=jnp.int32)
    means = group_sums / group_sizes
    spreads = group_squares / group_sizes - means * means
    own_mean = jnp.sum(jnp.where(own_hot, means, 0.0))
    own_spread = jnp.sum(jnp.where(own_hot, spreads, 0.0))
    advantage = (rewards[0].astype(F32) - own_mean) / jnp.sqrt(jnp.maximum(own_spread, 1.0))

    count_high = jnp.floor(counts_here / 64.0)
    count_tail = jnp.stack([count_high, counts_here - 64.0 * count_high])
    count_tail = jnp.pad(count_tail, (0, PADDED - D - 2)).astype(BF16)
    tails = jnp.broadcast_to(count_tail[None], (2 * SLOTS, PADDED - D))
    both = jnp.concatenate([jnp.concatenate([normed, upstream_slots], axis=0), tails], axis=1)
    at = jnp.arange(2 * SLOTS)
    source = (at // SLOTS) * CAP + at % CAP + jnp.where(at % SLOTS >= CAP, SLOTS, 0)
    arrange = (source[:, None] == at[None, :]).astype(BF16)
    by_expert = dot32(arrange, both).astype(BF16).reshape(EW, 1, 2 * CAP, PADDED)
    query_late, normed_late, route_late, upstream_rows, pick_low, by_expert, row_late, col_late = (
        lax.optimization_barrier(
            (
                query_rows,
                normed,
                route_rows,
                upstream_rows,
                pick_low,
                by_expert,
                row_index,
                col_index,
            )
        )
    )
    pick = pick_low > 0
    same = dot_last(pick_low, pick_low)
    primary = jnp.sum(jnp.tril(same, -1), axis=1) == 0
    place = jnp.where(primary[:, None], pick, False)
    taken = jnp.any(pick, axis=0)
    outgoing = jnp.broadcast_to(by_expert, (EW, pairs // EW, 2 * CAP, PADDED))
    came = exchange(outgoing.reshape(pairs, 2 * CAP, PADDED), "pair")

    back = experts_step(came.reshape(pairs * 2 * CAP, PADDED), *blocks)
    back, mask_late = lax.optimization_barrier(
        (back.reshape(pairs, CAP, PADDED), mask_row)
    )
    mask_late = mask_late.astype(F32)
    back = exchange(back, "pair")

    masked = jnp.where(mask_late[:, None] > 0.0, upstream_rows, jnp.zeros_like(upstream_rows))
    grad_attended = jnp.where(taken[:, None], 0.0, dot_last(masked, out_full)).astype(BF16)
    came, grad_attended = lax.optimization_barrier((came, grad_attended))
    count_parts = jnp.sum(came[:, 0, D : D + 2].astype(F32), axis=0)
    token_total = count_parts[0] * 64.0 + count_parts[1]
    token_scale = -advantage * all_tokens / token_total
    loss_weight = token_scale * mask_late
    probs, sink_probs = head_scores(
        query_late, keys_here, head_sink_logits, visible(row_late, col_late)
    )
    grad_prob, spread = head_spread(probs, values_here, grad_attended)
    back, grad_prob, spread = lax.optimization_barrier((back, grad_prob, spread))
    dense_sinks = jnp.sum(sink_probs * spread, axis=2).reshape(QUERY_HEADS) * token_scale
    summed = jnp.sum(back.reshape(EW, pairs // EW, CAP, PADDED).astype(F32), axis=1)
    summed = summed.reshape(SLOTS, PADDED)
    share_slots = jnp.sum(summed[:, D : D + 3], axis=1)

    logits = dot32(normed_late, router)
    route_slots = dot32(pick_low, route_late.astype(BF16)).astype(jnp.int32)
    route_hot = route_slots[:, :, None] == jnp.arange(EXPERTS, dtype=jnp.int32)
    route_logits = jnp.sum(jnp.where(route_hot, logits[:, None, :], 0.0), axis=2)
    raised = jnp.exp(route_logits)
    route_weights = raised / jnp.sum(raised, axis=1, keepdims=True)
    weight_slots = jnp.sum(
        jnp.where(route_slots == slot_expert[:, None], route_weights, 0.0), axis=1
    )
    loss_slots = jnp.sum(jnp.where(pick, loss_weight[None, :], 0.0), axis=1)
    cot_slots = loss_slots[:, None] * upstream_slots.astype(F32)
    grad_rows = (weight_slots * loss_slots)[:, None] * summed[:, :D]
    grad_rows = dot32(same, grad_rows, precision=HIGHEST)
    grad_share = loss_slots * share_slots
    token_share = jnp.sum(
        same[:, :, None] * (grad_share[:, None] * (slot_expert[:, None] == window))[None], axis=1
    )
    grad_weights = jnp.sum(
        jnp.where(route_slots[:, :, None] == window, token_share[:, None, :], 0.0), axis=2
    )
    grad_route = route_weights * (
        grad_weights - jnp.sum(route_weights * grad_weights, axis=1, keepdims=True)
    )
    grad_logits = jnp.sum(jnp.where(route_hot, grad_route[:, :, None], 0.0), axis=1).astype(BF16)
    grad_normed = dot_last(grad_logits, router) + grad_rows
    grad_unit = grad_normed * norm_gain[None, :]
    grad_slots = cot_slots + inv_rms * (
        grad_unit - unit_rows * jnp.mean(grad_unit * unit_rows, axis=1, keepdims=True)
    )
    grad_slots = jnp.where(primary[:, None], grad_slots, 0.0).astype(BF16)

    attended_grad_slots = dot_last(grad_slots, out_full).astype(BF16)
    slot_prob, slot_spread = head_spread(probs_slots, values_here, attended_grad_slots)
    slot_sinks = jnp.sum(sink_slots * slot_spread, axis=2).reshape(QUERY_HEADS)
    sinks = jnp.pad(-(dense_sinks + slot_sinks), (0, 128 - QUERY_HEADS))[None]
    sinks = to_all(sinks, ("core", "dp"))
    sinks, slot_prob, grad_prob, upstream_rows = lax.optimization_barrier(
        (jnp.sum(sinks, axis=0), slot_prob, grad_prob, upstream_rows)
    )
    sinks = to_all(sinks, ("pair", "half"))
    sinks = jnp.sum(sinks, axis=0)

    grad_q, grad_k, grad_v = head_grads(
        probs, grad_prob, spread, query_late, keys_here, grad_attended, token_scale
    )
    slot_q, slot_k, slot_v = head_grads(
        probs_slots, slot_prob, slot_spread, query_slots, keys_here, attended_grad_slots, 1.0
    )
    grad_k = grad_k + slot_k
    grad_v = grad_v + slot_v
    onward = jnp.concatenate([grad_k[:WINDOW], grad_v[:WINDOW]], axis=1).astype(BF16)
    onward = along_seq(onward, -1).astype(F32)
    grad_key_rows = (grad_k[WINDOW:] + onward[:, :kv_width]).astype(BF16)
    grad_value_rows = (grad_v[WINDOW:] + onward[:, kv_width:]).astype(BF16)
    cot_rows = (loss_weight[:, None] * upstream_rows.astype(F32)).astype(BF16)
    put = place.astype(BF16)
    by_token = (((0,), (0,)), ((), ()))
    grad_residual = jnp.where(
        taken[:, None],
        lax.dot_general(put, grad_slots, by_token, preferred_element_type=F32).astype(BF16),
        cot_rows,
    )
    grad_q = jnp.where(
        taken[:, None],
        lax.dot_general(put, slot_q, by_token, preferred_element_type=F32).astype(BF16),
        grad_q,
    )
    return (
        grad_q[None],
        grad_key_rows[None],
        grad_value_rows[None],
        grad_residual[None],
        sinks[0, :QUERY_HEADS],
    )


def solution(mesh):
    seq, dp = mesh.shape["seq"], mesh.shape["dp"]
    split = Mesh(mesh.devices.reshape(seq // 4, 2, 2, dp), (*SEQ, "dp"))
    whole = SEQ

    return jax.shard_map(
        shards,
        mesh=split,
        in_specs=(
            P("dp", whole, None),
            P("dp", whole, None),
            P("dp", whole, None),
            P(),
            P("dp", whole, None),
            P("dp", None),
            P(),
            P(),
            P("dp", whole),
            P("dp", whole),
            P("dp", whole),
            P("dp", whole, None),
            P("dp"),
            P("dp"),
            P("dp", whole),
            P("dp", whole, None),
        ),
        out_specs=(
            P("dp", whole, None),
            P("dp", whole, None),
            P("dp", whole, None),
            P("dp", whole, None),
            P(),
        ),
        check_vma=False,
    )
```
